512 devices in a mesh: gx: 64 (over z, x), gy: 8 (over y, core).
Axes of the slice: x: 4, y: 4, z: 16, core: 2. Of those that a mesh axis runs over, the one named last changes fastest.
Arguments:
- blocks_a: bfloat16 [64, 64, 5, 4096], P('gx', 'gy'), may hold values from -0.75 to 0.75
- prolong: bfloat16 [64, 64, 4096], P('gx', 'gy'), may hold values from -1.5 to 1.5
- aggregate: int32 [64, 64], P('gx', 'gy'), may hold values from 0 to 63, as said below
- coupling_slot: int32 [64, 64, 5], P('gx', 'gy'), may hold values from 0 to 7
Outputs:
- coarse: float32 [64, 8, 8, 4096], P('gx', 'gy')
The draws below stay inside these ranges and needn't reach their ends.
Inputs may be any that keep to these rules, and one draw needn't show every extreme that they name: The aggregate a of an element is held by the device of gx index a // 1 in the element's own gy column. Of the elements of any one device at most 2 have aggregates held by one gx index, and on every device some gx index holds exactly 2 of them.
All inputs are finite; a program needn't handle non-finite values.
Results may differ from the reference program's by a relative error of at most 0.004.
Values may be sent and summed in bfloat16 or wider, within the bound.
No kernel may reach another device: no remote copies, remote signals or barrier semaphores. Data moves between devices by JAX's collectives and lax.ppermute only.
A program may use at most 64 MiB of HBM per device.

```python
import jax
import jax.numpy as jnp
from jax import lax

B = 64
K = 5
CS = 8
CX = 1
CY = 8
AGG_DEV = 1
CAP = 2
NX = 64
NY = 64
AGGS = 64
N_GX = 64
N_GY = 8


def draw_aggregate(key, part):
    devices = N_GX * N_GY
    per_device = CX * CY
    eligible_clusters = N_GX * CAP
    prospective_cluster = (jnp.arange(eligible_clusters, dtype=jnp.int32) // CAP).astype(jnp.int32)
    base = jax.random.fold_in(key, 7001)

    def one_device(index):
        subkey = jax.random.fold_in(base, index)
        keys = jax.random.split(subkey, 5)
        likeliest_cluster = jax.random.randint(keys[0], (), 0, N_GX)
        inclination_factor = jax.random.randint(keys[1], (N_GX,), 0, 4)
        stochastic_perturbation = jax.random.randint(keys[2], (eligible_clusters,), 0, 65536)
        kinship_increment = (prospective_cluster == likeliest_cluster).astype(jnp.int32) * 262144
        selection_merit = (stochastic_perturbation + inclination_factor[prospective_cluster] * 65536 + kinship_increment) * eligible_clusters + jnp.arange(eligible_clusters, dtype=jnp.int32)
        chosen = lax.top_k(selection_merit, per_device)[1]
        owners = jax.random.permutation(keys[3], prospective_cluster[chosen])
        local_id = jax.random.randint(keys[4], (per_device,), 0, AGG_DEV)
        return owners * AGG_DEV + local_id
    table = jax.vmap(one_device)(jnp.arange(devices, dtype=jnp.int32))
    return table.reshape(N_GX, N_GY, CX, CY).transpose(0, 2, 1, 3).reshape(N_GX * CX, N_GY * CY).astype(jnp.int32)


def with_ends(array, own_key, low, largest):
    extent = array.shape
    place = [jax.random.randint(jax.random.fold_in(own_key, axis), (), 0, extent[axis]) for axis in range(len(extent))]
    array = array.at[tuple(place)].set(low)
    longest = extent.index(max(extent))
    place[longest] = (place[longest] + 1) % extent[longest]
    return array.at[tuple(place)].set(largest)


def levels(own_key, extent, cuts, least, largest):
    loudness, own = 1.0, jax.random.fold_in(own_key, 6)
    for dim, blocks in cuts:
        steps = jnp.exp(jax.random.uniform(jax.random.fold_in(own, dim), (blocks,), jnp.float32, least / len(cuts), largest / len(cuts)))
        loudness = loudness * jnp.repeat(steps, extent[dim] // blocks).reshape([-1 if axis == dim else 1 for axis in range(len(extent))])
    return loudness


def gaussian(own_key, extent, deviation, reach, cuts=(), kind=jnp.bfloat16):
    loudness = levels(own_key, extent, cuts, -0.22, 0.18) if cuts else 1.0
    entries = jax.random.normal(own_key, extent, jnp.float32) * deviation * loudness
    return jnp.minimum(jnp.maximum(entries, -reach), reach).astype(kind)


def setup_inputs(seed: int = 0) -> dict:
    key_of = jax.random.split(jax.random.key(seed), 5)
    blocks_a = gaussian(key_of[0], (NX, NY, K, B * B), B ** -0.5, 0.75, ((0, 64), (1, 8)))
    prolong = gaussian(key_of[1], (NX, NY, B * B), 0.25, 1.5, ((0, 64), (1, 8)))
    aggregate = draw_aggregate(jax.random.fold_in(key_of[4], 71), 0)
    coupling_slot = with_ends(jax.random.randint(key_of[3], (NX, NY, K), 0, CS), jax.random.fold_in(key_of[3], 1), 0, CS - 1).astype(jnp.int32)
    return {"blocks_a": blocks_a, "prolong": prolong, "aggregate": aggregate, "coupling_slot": coupling_slot}


def reference(blocks_a, prolong, aggregate, coupling_slot):
    block_len = B * B
    padded = jnp.pad(prolong, ((1, 1), (1, 1), (0, 0)))
    column_of = (jnp.arange(NY, dtype=jnp.int32) // CY).astype(jnp.int32)

    def row_step(coarse_flat, index):
        a_row = lax.dynamic_index_in_dim(blocks_a, index, 0, keepdims=False)
        window = lax.dynamic_slice_in_dim(padded, index, 3, 0)
        beside = jnp.stack([window[1, 1:-1], window[0, 1:-1], window[2, 1:-1], window[1, :-2], window[1, 2:]], axis=1)
        matrix_a = a_row.reshape(NY, K, B, B).astype(jnp.float32)
        matrix_p = beside.reshape(NY, K, B, B).astype(jnp.float32)
        product = jnp.einsum("jkab,jkbc->jkac", matrix_a, matrix_p, precision=lax.Precision.HIGHEST).astype(jnp.bfloat16)
        product = lax.optimization_barrier(product).astype(jnp.float32)
        own_block = window[1, 1:-1].reshape(NY, B, B).astype(jnp.float32)
        contribution = jnp.einsum("jba,jkbc->jkac", own_block, product, precision=lax.Precision.HIGHEST).astype(jnp.bfloat16)
        contribution = lax.optimization_barrier(contribution).astype(jnp.float32)
        agg_row = lax.dynamic_index_in_dim(aggregate, index, 0, keepdims=False).astype(jnp.int32)
        slot_row = lax.dynamic_index_in_dim(coupling_slot, index, 0, keepdims=False).astype(jnp.int32)
        target = ((agg_row * N_GY + column_of)[:, None] * CS + slot_row).astype(jnp.int32)
        coarse_flat = coarse_flat.at[target.reshape(-1)].add(contribution.reshape(NY * K, block_len))
        return coarse_flat, None

    start = jnp.zeros((AGGS * N_GY * CS, block_len), jnp.float32)
    coarse_flat, unused = lax.scan(row_step, start, jnp.arange(NX, dtype=jnp.int32))
    return coarse_flat.reshape(AGGS, N_GY, CS, block_len)
```

```python
import jax
import jax.numpy as jnp
from jax import lax
from jax.experimental import pallas as pl
from jax.experimental.pallas import tpu as pltpu
from jax.sharding import PartitionSpec as P

B = 64
K = 5
CS = 8
E = 8
Q = 32
LANES = 128
NX = 4
NZ = 16


F32 = jnp.float32
BF16 = jnp.bfloat16


VMEM = pl.BlockSpec(memory_space=pltpu.VMEM)
SMEM = pl.BlockSpec(memory_space=pltpu.SMEM)


def low_half(shape):
    return lax.broadcasted_iota(jnp.int32, shape, len(shape) - 1) < B


def products_kernel(a_ref, p_ref, up_ref, dn_ref, lf_ref, rt_ref, out_ref, a2, wd, p2, t2):
    low8 = low_half((E, LANES))
    for k in range(K):
        for q in range(Q):
            x = a_ref[k, :, LANES * q : LANES * (q + 1)].astype(F32)
            a2[pl.ds(k * E * Q + q, E, stride=Q), :] = x
    for number, ref in enumerate((p_ref, up_ref, dn_ref)):
        for q in range(Q):
            x = ref[:, LANES * q : LANES * (q + 1)].astype(F32)
            r = pltpu.roll(x, B, 1)
            if number == 0:
                p2[pl.ds(q, E, stride=Q), :] = x
            base = number * E * B
            wd[pl.ds(base + 2 * q, E, stride=B), :] = jnp.where(low8, x, r)
            wd[pl.ds(base + 2 * q + 1, E, stride=B), :] = jnp.where(low8, r, x)
    for number, ref, row in ((3 * E, lf_ref, E - 1), (3 * E + 1, rt_ref, 0)):
        for q in range(Q):
            x = ref[:, LANES * q : LANES * (q + 1)].astype(F32)
            r = pltpu.roll(x, B, 1)
            even = jnp.where(low8, x, r)
            odd = jnp.where(low8, r, x)
            wd[number * B + 2 * q : number * B + 2 * q + 1, :] = even[row : row + 1]
            wd[number * B + 2 * q + 1 : number * B + 2 * q + 2, :] = odd[row : row + 1]
    low64 = low_half((B, LANES))

    def multiply(number, users):
        twice = wd[number * B : (number + 1) * B, :]
        zero = jnp.zeros_like(twice)
        weights = jnp.concatenate(
            [jnp.where(low64, twice, zero), jnp.where(low64, zero, twice)], axis=0
        ).astype(BF16)
        rows = [a2[(k * E + e) * Q : (k * E + e + 1) * Q, :] for e, k in users]
        left = (rows[0] if len(rows) == 1 else jnp.concatenate(rows, axis=0)).astype(BF16)
        result = jnp.dot(left, weights, preferred_element_type=F32).astype(BF16)
        for place, (e, k) in enumerate(users):
            t2[e, :, LANES * k : LANES * (k + 1)] = result[place * Q : (place + 1) * Q]

    for e in range(E):
        users = [(e, 0)]
        if e + 1 < E:
            users.append((e + 1, 3))
        if e > 0:
            users.append((e - 1, 4))
        multiply(e, users)
        multiply(E + e, [(e, 1)])
        multiply(2 * E + e, [(e, 2)])
    multiply(3 * E, [(0, 3)])
    multiply(3 * E + 1, [(E - 1, 4)])

    low32 = low_half((Q, LANES))
    for e in range(E):
        pt = jnp.transpose(p2[e * Q : (e + 1) * Q, :]).astype(BF16)
        g = jnp.dot(pt, t2[e], preferred_element_type=F32)
        for k in range(K):
            u = g[:B, LANES * k : LANES * (k + 1)]
            v = g[B:, LANES * k : LANES * (k + 1)]
            first = u[:Q] + pltpu.roll(v[:Q], B, 1)
            second = pltpu.roll(u[Q:], B, 1) + v[Q:]
            out_ref[e * K + k] = jnp.where(low32, first, second).astype(BF16)


def products(a, p, up, dn, lf, rt):
    return pl.pallas_call(
        products_kernel,
        out_shape=jax.ShapeDtypeStruct((E * K, Q, LANES), BF16),
        in_specs=[VMEM] * 6,
        out_specs=VMEM,
        scratch_shapes=[
            pltpu.VMEM((K * E * Q, LANES), F32),
            pltpu.VMEM(((3 * E + 2) * B, LANES), F32),
            pltpu.VMEM((E * Q, LANES), F32),
            pltpu.VMEM((E, Q, K * LANES), BF16),
        ],
        name="products",
    )(a, p, up, dn, lf, rt)


PLUS_1 = (1, 5, 9, 13)
MINUS_1 = (15, 3, 7, 11)
PLUS_2 = (2, 6)
MINUS_2 = (14, 10)
STAY = (0, 4, 8, 12)
X_SHIFTS = (0, 3, 1, 2)


def table_kernel(meta_ref, pos_ref, c0, c1, c2, c3, p1, m1, p2, m2, own, tab):
    for block in range(NZ * CS):
        tab[block] = jnp.zeros((Q, LANES), F32)
    z = pos_ref[0]
    x = pos_ref[1]
    for ref, shift in zip((c0, c1, c2, c3), X_SHIFTS):
        source = (x + shift) & (NX - 1)

        def take(e, carry, ref=ref, source=source):
            owner = meta_ref[source, e]

            @pl.when((owner & (NX - 1)) == x)
            def _():
                distance = ((owner >> 2) - z) & (NZ - 1)
                for k in range(K):
                    row = distance * CS + meta_ref[source, E + k * E + e]
                    tab[row] += ref[e * K + k].astype(F32)

            return carry

        lax.fori_loop(0, E, take, 0)
    for ref, distances in ((p1, PLUS_1), (m1, MINUS_1), (p2, PLUS_2), (m2, MINUS_2), (own, STAY)):
        for place, distance in enumerate(distances):
            for slot in range(CS):
                ref[place * CS + slot] = tab[distance * CS + slot].astype(ref.dtype)


def table(meta, pos, c0, c1, c2, c3):
    def rows(blocks, dtype):
        return jax.ShapeDtypeStruct((blocks * CS, Q, LANES), dtype)

    return pl.pallas_call(
        table_kernel,
        out_shape=(rows(4, BF16), rows(4, BF16), rows(2, BF16), rows(2, BF16), rows(4, F32)),
        in_specs=[SMEM, SMEM] + [VMEM] * 4,
        out_specs=(VMEM,) * 5,
        scratch_shapes=[pltpu.VMEM((NZ * CS, Q, LANES), F32)],
        name="table",
    )(meta, pos, c0, c1, c2, c3)


def partial_kernel(own, p1, m1, p2, m2, r0, r1, r2, r3):
    def part(ref, place):
        return ref[place * CS : (place + 1) * CS].astype(F32)

    r0[...] = part(own, 0) + part(p1, 0) + part(m1, 0) + part(p2, 0) + part(m2, 0)
    r1[...] = (part(own, 1) + part(p1, 1) + part(m1, 1) + part(p2, 1)).astype(BF16)
    r2[...] = (part(own, 2) + part(p1, 2) + part(m1, 2)).astype(BF16)
    r3[...] = (part(own, 3) + part(p1, 3) + part(m1, 3) + part(m2, 1)).astype(BF16)


def partial_sums(own, p1, m1, p2, m2):
    def rows(dtype):
        return jax.ShapeDtypeStruct((CS, Q, LANES), dtype)

    return pl.pallas_call(
        partial_kernel,
        out_shape=(rows(F32), rows(BF16), rows(BF16), rows(BF16)),
        in_specs=[VMEM] * 5,
        out_specs=(VMEM,) * 4,
        name="partial_sums",
    )(own, p1, m1, p2, m2)


def finish_kernel(r0, r1, r2, r3, out_ref, total):
    for slot in range(CS):
        total[slot * Q : (slot + 1) * Q, :] = (
            r0[slot] + r1[slot].astype(F32) + r2[slot].astype(F32) + r3[slot].astype(F32)
        )
    low8 = low_half((CS, LANES))
    for pair in range(Q // 2):
        even = total[pl.ds(2 * pair, CS, stride=Q), :]
        odd = total[pl.ds(2 * pair + 1, CS, stride=Q), :]
        out_ref[:, LANES * pair : LANES * (pair + 1)] = jnp.where(low8, even, pltpu.roll(odd, B, 1))
        place = pair + Q // 2
        out_ref[:, LANES * place : LANES * (place + 1)] = jnp.where(
            low8, pltpu.roll(even, B, 1), odd
        )


def finish(r0, r1, r2, r3):
    return pl.pallas_call(
        finish_kernel,
        out_shape=jax.ShapeDtypeStruct((CS, B * B), F32),
        in_specs=[VMEM] * 4,
        out_specs=VMEM,
        scratch_shapes=[pltpu.VMEM((CS * Q, LANES), F32)],
        name="finish",
    )(r0, r1, r2, r3)


def along_x(shift):
    return [(NX * z + x, NX * z + (x + shift) % NX) for z in range(NZ) for x in range(NX)]


def along_z(shift):
    return [(NX * z + x, NX * ((z + shift) % NZ) + x) for z in range(NZ) for x in range(NX)]


def body(blocks_a, prolong, aggregate, coupling_slot):
    count_x = lax.axis_size("gx")
    count_y = lax.axis_size("gy")
    own = prolong.reshape(E, B * B)
    up = lax.ppermute(own, "gx", [(i, i + 1) for i in range(count_x - 1)])
    down = lax.ppermute(own, "gx", [(i + 1, i) for i in range(count_x - 1)])
    left = lax.ppermute(own, "gy", [(i, i + 1) for i in range(count_y - 1)])
    right = lax.ppermute(own, "gy", [(i + 1, i) for i in range(count_y - 1)])
    slots = coupling_slot.reshape(E, K).T.reshape(E * K)
    mine = jnp.concatenate(
        [aggregate.reshape(E), slots, jnp.zeros((LANES - E - E * K,), jnp.int32)]
    )
    groups = [[NX * z + x for x in range(NX)] for z in range(NZ)]
    meta = lax.all_to_all(
        jnp.broadcast_to(mine[None], (NX, LANES)),
        "gx",
        0,
        0,
        axis_index_groups=groups,
        tiled=True,
    )
    index = lax.axis_index("gx")
    pos = jnp.stack([index // NX, index % NX]).astype(jnp.int32)
    matrix_a = blocks_a.reshape(E, K, B * B).transpose(1, 0, 2)
    c0 = products(matrix_a, own, up, down, left, right)
    c1 = lax.ppermute(c0, "gx", along_x(1))
    c2 = lax.ppermute(c0, "gx", along_x(-1))
    c3 = lax.ppermute(c0, "gx", along_x(2))
    p1, m1, p2, m2, stay = table(meta, pos, c0, c1, c2, c3)
    p2 = lax.ppermute(p2, "gx", along_z(2))
    m2 = lax.ppermute(m2, "gx", along_z(-2))
    p1 = lax.ppermute(p1, "gx", along_z(1))
    m1 = lax.ppermute(m1, "gx", along_z(-1))
    r0, r1, r2, r3 = partial_sums(stay, p1, m1, p2, m2)
    r2 = lax.ppermute(r2, "gx", along_z(8))
    r1 = lax.ppermute(r1, "gx", along_z(4))
    r3 = lax.ppermute(r3, "gx", along_z(-4))
    return finish(r0, r1, r2, r3).reshape(1, 1, CS, B * B)


def solution(mesh):
    return jax.shard_map(
        body,
        mesh=mesh,
        in_specs=(
            P("gx", "gy", None, None),
            P("gx", "gy", None),
            P("gx", "gy"),
            P("gx", "gy", None),
        ),
        out_specs=P("gx", "gy", None, None),
        check_vma=False,
    )
```

```python
import jax
import jax.numpy as jnp
from jax import lax
from jax.experimental import pallas as pl
from jax.experimental.pallas import tpu as pltpu
from jax.sharding import PartitionSpec as P

B = 64
K = 5
CS = 8
E = 8
Q = 32
LANES = 128
NX = 4
NZ = 16


F32 = jnp.float32
BF16 = jnp.bfloat16


VMEM = pl.BlockSpec(memory_space=pltpu.VMEM)
SMEM = pl.BlockSpec(memory_space=pltpu.SMEM)


def low_half(shape):
    return lax.broadcasted_iota(jnp.int32, shape, len(shape) - 1) < B


def products_kernel(agg_ref, slot_ref, a_ref, p_ref, xa, xb, ya, yb, out_ref, a2, wd, p2, t2):
    low8 = low_half((E, LANES))
    for k in range(K):
        for q in range(Q):
            x = a_ref[k, :, LANES * q : LANES * (q + 1)].astype(F32)
            a2[pl.ds(k * E * Q + q, E, stride=Q), :] = x
    for number, ref in enumerate((p_ref, xa, xb, ya, yb)):
        for q in range(Q):
            x = ref[:, LANES * q : LANES * (q + 1)].astype(F32)
            r = pltpu.roll(x, B, 1)
            if number == 0:
                p2[pl.ds(q, E, stride=Q), :] = x
            base = number * E * B
            wd[pl.ds(base + 2 * q, E, stride=B), :] = jnp.where(low8, x, r)
            wd[pl.ds(base + 2 * q + 1, E, stride=B), :] = jnp.where(low8, r, x)
    low64 = low_half((B, LANES))
    odd_x = lax.axis_index("gx") & 1
    odd_y = lax.axis_index("gy") & 1

    def multiply(number, users):
        start = number * B if isinstance(number, int) else pl.multiple_of(number * B, B)
        twice = wd[pl.ds(start, B), :]
        zero = jnp.zeros_like(twice)
        weights = jnp.concatenate(
            [jnp.where(low64, twice, zero), jnp.where(low64, zero, twice)], axis=0
        ).astype(BF16)
        rows = [a2[(k * E + e) * Q : (k * E + e + 1) * Q, :] for e, k in users]
        left = (rows[0] if len(rows) == 1 else jnp.concatenate(rows, axis=0)).astype(BF16)
        result = jnp.dot(left, weights, preferred_element_type=F32).astype(BF16)
        for place, (e, k) in enumerate(users):
            t2[e, :, LANES * k : LANES * (k + 1)] = result[place * Q : (place + 1) * Q]

    for e in range(E):
        users = [(e, 0)]
        if e + 1 < E:
            users.append((e + 1, 3))
        if e > 0:
            users.append((e - 1, 4))
        multiply(e, users)
        multiply(2 * E - odd_x * E + e, [(e, 1)])
        multiply(E + odd_x * E + e, [(e, 2)])
    multiply(4 * E - odd_y * E + E - 1, [(0, 3)])
    multiply(3 * E + odd_y * E, [(E - 1, 4)])

    low32 = low_half((Q, LANES))
    for e in range(E):
        pt = jnp.transpose(p2[e * Q : (e + 1) * Q, :]).astype(BF16)
        g = jnp.dot(pt, t2[e], preferred_element_type=F32)
        for k in range(K):
            u = g[:B, LANES * k : LANES * (k + 1)]
            v = g[B:, LANES * k : LANES * (k + 1)]
            first = u[:Q] + pltpu.roll(v[:Q], B, 1)
            second = pltpu.roll(u[Q:], B, 1) + v[Q:]
            block = jnp.where(low32, first, second).astype(BF16)
            for d in range(NX):
                out_ref[d, e * K + k] = block
    lane = lax.broadcasted_iota(jnp.int32, (E, LANES), 1)
    tags = jnp.zeros((E, LANES), jnp.int32)
    for e in range(E):
        tags = jnp.where(lane == e, agg_ref[0, e], tags)
        for k in range(K):
            tags = jnp.where(lane == E + k * E + e, slot_ref[k, 0, e], tags)
    tags = jnp.concatenate([tags.astype(F32)] * (Q // E), axis=0).astype(BF16)
    for d in range(NX):
        out_ref[d, E * K] = tags


def products(agg, slot, a, p, xa, xb, ya, yb):
    return pl.pallas_call(
        products_kernel,
        out_shape=jax.ShapeDtypeStruct((NX, E * K + 1, Q, LANES), BF16),
        in_specs=[SMEM] * 2 + [VMEM] * 6,
        out_specs=VMEM,
        scratch_shapes=[
            pltpu.VMEM((K * E * Q, LANES), F32),
            pltpu.VMEM((5 * E * B, LANES), F32),
            pltpu.VMEM((E * Q, LANES), F32),
            pltpu.VMEM((E, Q, K * LANES), BF16),
        ],
        name="products",
    )(agg, slot, a, p, xa, xb, ya, yb)


NL = 4


def table_kernel(c_ref, out_ref, tab, tags, scalars, sem):
    for source in range(NX):
        row = c_ref[source, E * K, :E].astype(F32).astype(jnp.int32)
        tags[source : source + 1, :] = row[:1]
    copy = pltpu.make_async_copy(tags, scalars, sem)
    copy.start()
    for block in range(NZ * CS):
        tab[block] = jnp.zeros((Q, LANES), F32)
    copy.wait()
    x = lax.axis_index("gx") & (NX - 1)
    for source in range(NX):

        def take(e, carry, source=source):
            owner = scalars[source, e]

            @pl.when((owner & (NX - 1)) == x)
            def _():
                z = owner >> 2
                base = ((z & (NL - 1)) * NL + (z >> 2)) * CS
                for k in range(K):
                    row = base + scalars[source, E + k * E + e]
                    tab[row] += c_ref[source, e * K + k].astype(F32)

            return carry

        lax.fori_loop(0, E, take, 0)
    for block in range(NZ * CS):
        out_ref[block // (NL * CS), block % (NL * CS)] = tab[block].astype(BF16)


def table(c):
    return pl.pallas_call(
        table_kernel,
        out_shape=jax.ShapeDtypeStruct((NL, NL * CS, Q, LANES), BF16),
        in_specs=[VMEM],
        out_specs=VMEM,
        scratch_shapes=[
            pltpu.VMEM((NZ * CS, Q, LANES), F32),
            pltpu.VMEM((NX, LANES), jnp.int32),
            pltpu.SMEM((NX, LANES), jnp.int32),
            pltpu.SemaphoreType.DMA,
        ],
        name="table",
    )(c)


def partial_kernel(t_ref, out_ref):
    for block in range(NL * CS):
        total = t_ref[0, block].astype(F32)
        for source in range(1, NL):
            total += t_ref[source, block].astype(F32)
        out_ref[block // CS, block % CS] = total.astype(BF16)


def partial_sums(t):
    return pl.pallas_call(
        partial_kernel,
        out_shape=jax.ShapeDtypeStruct((NL, CS, Q, LANES), BF16),
        in_specs=[VMEM],
        out_specs=VMEM,
        name="partial_sums",
    )(t)


def finish_kernel(r_ref, out_ref, total):
    for slot in range(CS):
        row = r_ref[0, slot].astype(F32)
        for source in range(1, NL):
            row += r_ref[source, slot].astype(F32)
        total[slot * Q : (slot + 1) * Q, :] = row
    low8 = low_half((CS, LANES))
    for pair in range(Q // 2):
        even = total[pl.ds(2 * pair, CS, stride=Q), :]
        odd = total[pl.ds(2 * pair + 1, CS, stride=Q), :]
        out_ref[:, LANES * pair : LANES * (pair + 1)] = jnp.where(low8, even, pltpu.roll(odd, B, 1))
        place = pair + Q // 2
        out_ref[:, LANES * place : LANES * (place + 1)] = jnp.where(
            low8, pltpu.roll(even, B, 1), odd
        )


def finish(r):
    return pl.pallas_call(
        finish_kernel,
        out_shape=jax.ShapeDtypeStruct((CS, B * B), F32),
        in_specs=[VMEM],
        out_specs=VMEM,
        scratch_shapes=[pltpu.VMEM((CS * Q, LANES), F32)],
        name="finish",
    )(r)


def swaps(count, first):
    pairs = [(i, i + 1) for i in range(first, count - 1, 2)]
    return pairs + [(j, i) for i, j in pairs]


X_GROUPS = [[NX * z + x for x in range(NX)] for z in range(NZ)]
FAR_GROUPS = [[NX * (NL * h + l) + x for h in range(NL)] for l in range(NL) for x in range(NX)]


def near_groups(count_y):
    groups = []
    for y in range(count_y):
        for h in range(NL):
            for x in range(NX):
                z = [NL * h + l + (NL if y % 2 and l < NL // 2 else 0) for l in range(NL)]
                groups.append([(NX * (place % NZ) + x) * count_y + y for place in z])
    return groups


def exchange(value, groups):
    return lax.all_to_all(value, "gx", 0, 0, axis_index_groups=groups, tiled=True)


def body(blocks_a, prolong, aggregate, coupling_slot):
    count_x = lax.axis_size("gx")
    count_y = lax.axis_size("gy")
    own = prolong.reshape(E, B * B)
    ya = lax.ppermute(own, "gy", swaps(count_y, 0))
    yb = lax.ppermute(own, "gy", swaps(count_y, 1))
    xa = lax.ppermute(own, "gx", swaps(count_x, 0))
    xb = lax.ppermute(own, "gx", swaps(count_x, 1))
    matrix_a = blocks_a.reshape(E, K, B * B).transpose(1, 0, 2)
    slots = coupling_slot.transpose(2, 0, 1)
    c = exchange(products(aggregate, slots, matrix_a, own, xa, xb, ya, yb), X_GROUPS)
    t = lax.all_to_all(
        table(c), ("gx", "gy"), 0, 0, axis_index_groups=near_groups(count_y), tiled=True
    )
    return finish(exchange(partial_sums(t), FAR_GROUPS)).reshape(1, 1, CS, B * B)


def solution(mesh):
    return jax.shard_map(
        body,
        mesh=mesh,
        in_specs=(
            P("gx", "gy", None, None),
            P("gx", "gy", None),
            P("gx", "gy"),
            P("gx", "gy", None),
        ),
        out_specs=P("gx", "gy", None, None),
        check_vma=False,
    )
```

```python
import jax
import jax.numpy as jnp
from jax import lax
from jax.experimental import pallas as pl
from jax.experimental.pallas import tpu as pltpu
from jax.sharding import PartitionSpec as P

B = 64
K = 5
CS = 8
E = 8
Q = 32
LANES = 128
NX = 4
NZ = 16


F32 = jnp.float32
BF16 = jnp.bfloat16


VMEM = pl.BlockSpec(memory_space=pltpu.VMEM)
SMEM = pl.BlockSpec(memory_space=pltpu.SMEM)


PARAMS = pltpu.CompilerParams(vmem_limit_bytes=24 * 1024 * 1024)


def near(value):
    return pltpu.with_memory_space_constraint(value, pltpu.VMEM)


def low_half(shape):
    return lax.broadcasted_iota(jnp.int32, shape, len(shape) - 1) < B


def products_kernel(agg_ref, slot_ref, a_ref, p_ref, xa, xb, ya, yb, out_ref, a2, wd, p2, t2):
    low8 = low_half((E, LANES))
    for k in range(K):
        for q in range(Q):
            x = a_ref[k, :, LANES * q : LANES * (q + 1)].astype(F32)
            a2[pl.ds(k * E * Q + q, E, stride=Q), :] = x
    for number, ref in enumerate((p_ref, xa, xb, ya, yb)):
        for q in range(Q):
            x = ref[:, LANES * q : LANES * (q + 1)].astype(F32)
            r = pltpu.roll(x, B, 1)
            if number == 0:
                p2[pl.ds(q, E, stride=Q), :] = x
            base = number * E * B
            wd[pl.ds(base + 2 * q, E, stride=B), :] = jnp.where(low8, x, r)
            wd[pl.ds(base + 2 * q + 1, E, stride=B), :] = jnp.where(low8, r, x)
    low64 = low_half((B, LANES))
    odd_x = lax.axis_index("gx") & 1
    odd_y = lax.axis_index("gy") & 1

    def multiply(number, users):
        start = number * B if isinstance(number, int) else pl.multiple_of(number * B, B)
        twice = wd[pl.ds(start, B), :]
        zero = jnp.zeros_like(twice)
        weights = jnp.concatenate(
            [jnp.where(low64, twice, zero), jnp.where(low64, zero, twice)], axis=0
        ).astype(BF16)
        rows = [a2[(k * E + e) * Q : (k * E + e + 1) * Q, :] for e, k in users]
        left = (rows[0] if len(rows) == 1 else jnp.concatenate(rows, axis=0)).astype(BF16)
        result = jnp.dot(left, weights, preferred_element_type=F32).astype(BF16)
        for place, (e, k) in enumerate(users):
            t2[e, :, LANES * k : LANES * (k + 1)] = result[place * Q : (place + 1) * Q]

    for e in range(E):
        users = [(e, 0)]
        if e + 1 < E:
            users.append((e + 1, 3))
        if e > 0:
            users.append((e - 1, 4))
        multiply(e, users)
        multiply(2 * E - odd_x * E + e, [(e, 1)])
        multiply(E + odd_x * E + e, [(e, 2)])
    multiply(4 * E - odd_y * E + E - 1, [(0, 3)])
    multiply(3 * E + odd_y * E, [(E - 1, 4)])

    low32 = low_half((Q, LANES))
    for e in range(E):
        pt = jnp.transpose(p2[e * Q : (e + 1) * Q, :]).astype(BF16)
        g = jnp.dot(pt, t2[e], preferred_element_type=F32)
        for k in range(K):
            u = g[:B, LANES * k : LANES * (k + 1)]
            v = g[B:, LANES * k : LANES * (k + 1)]
            first = u[:Q] + pltpu.roll(v[:Q], B, 1)
            second = pltpu.roll(u[Q:], B, 1) + v[Q:]
            block = jnp.where(low32, first, second).astype(BF16)
            for d in range(NX):
                out_ref[d, e * K + k] = block
    lane = lax.broadcasted_iota(jnp.int32, (E, LANES), 1)
    tags = jnp.zeros((E, LANES), jnp.int32)
    for e in range(E):
        tags = jnp.where(lane == e, agg_ref[0, e], tags)
        for k in range(K):
            tags = jnp.where(lane == E + k * E + e, slot_ref[k, 0, e], tags)
    tags = jnp.concatenate([tags.astype(F32)] * (Q // E), axis=0).astype(BF16)
    for d in range(NX):
        out_ref[d, E * K] = tags


def products(agg, slot, a, p, xa, xb, ya, yb):
    return pl.pallas_call(
        products_kernel,
        out_shape=pltpu.VMEM((NX, E * K + 1, Q, LANES), BF16),
        in_specs=[SMEM] * 2 + [VMEM] * 6,
        out_specs=VMEM,
        scratch_shapes=[
            pltpu.VMEM((K * E * Q, LANES), F32),
            pltpu.VMEM((5 * E * B, LANES), F32),
            pltpu.VMEM((E * Q, LANES), F32),
            pltpu.VMEM((E, Q, K * LANES), BF16),
        ],
        compiler_params=PARAMS,
        name="products",
    )(agg, slot, a, p, *map(near, (xa, xb, ya, yb)))


NL = 4


def table_kernel(c_ref, out_ref, tab, tags, scalars, sem):
    for source in range(NX):
        row = c_ref[source, E * K, :E].astype(F32).astype(jnp.int32)
        tags[source : source + 1, :] = row[:1]
    copy = pltpu.make_async_copy(tags, scalars, sem)
    copy.start()
    for block in range(NZ * CS):
        tab[block] = jnp.zeros((Q, LANES), F32)
    copy.wait()
    x = lax.axis_index("gx") & (NX - 1)
    for source in range(NX):

        def take(e, carry, source=source):
            owner = scalars[source, e]

            @pl.when((owner & (NX - 1)) == x)
            def _():
                z = owner >> 2
                base = ((z & (NL - 1)) * NL + (z >> 2)) * CS
                for k in range(K):
                    row = base + scalars[source, E + k * E + e]
                    tab[row] += c_ref[source, e * K + k].astype(F32)

            return carry

        lax.fori_loop(0, E, take, 0)
    for block in range(NZ * CS):
        out_ref[block // (NL * CS), block % (NL * CS)] = tab[block].astype(BF16)


def table(c):
    return pl.pallas_call(
        table_kernel,
        out_shape=pltpu.VMEM((NL, NL * CS, Q, LANES), BF16),
        in_specs=[VMEM],
        out_specs=VMEM,
        scratch_shapes=[
            pltpu.VMEM((NZ * CS, Q, LANES), F32),
            pltpu.VMEM((NX, LANES), jnp.int32),
            pltpu.SMEM((NX, LANES), jnp.int32),
            pltpu.SemaphoreType.DMA,
        ],
        compiler_params=PARAMS,
        name="table",
    )(near(c))


def partial_kernel(t_ref, out_ref):
    for block in range(NL * CS):
        total = t_ref[0, block].astype(F32)
        for source in range(1, NL):
            total += t_ref[source, block].astype(F32)
        out_ref[block // CS, block % CS] = total.astype(BF16)


def partial_sums(t):
    return pl.pallas_call(
        partial_kernel,
        out_shape=pltpu.VMEM((NL, CS, Q, LANES), BF16),
        in_specs=[VMEM],
        out_specs=VMEM,
        compiler_params=PARAMS,
        name="partial_sums",
    )(near(t))


def finish_kernel(r_ref, out_ref, total):
    for slot in range(CS):
        row = r_ref[0, slot].astype(F32)
        for source in range(1, NL):
            row += r_ref[source, slot].astype(F32)
        total[slot * Q : (slot + 1) * Q, :] = row
    low8 = low_half((CS, LANES))
    for pair in range(Q // 2):
        even = total[pl.ds(2 * pair, CS, stride=Q), :]
        odd = total[pl.ds(2 * pair + 1, CS, stride=Q), :]
        out_ref[:, LANES * pair : LANES * (pair + 1)] = jnp.where(low8, even, pltpu.roll(odd, B, 1))
        place = pair + Q // 2
        out_ref[:, LANES * place : LANES * (place + 1)] = jnp.where(
            low8, pltpu.roll(even, B, 1), odd
        )


def finish(r):
    return pl.pallas_call(
        finish_kernel,
        out_shape=jax.ShapeDtypeStruct((CS, B * B), F32),
        in_specs=[VMEM],
        out_specs=VMEM,
        scratch_shapes=[pltpu.VMEM((CS * Q, LANES), F32)],
        compiler_params=PARAMS,
        name="finish",
    )(near(r))


def swaps(count, first):
    pairs = [(i, i + 1) for i in range(first, count - 1, 2)]
    return pairs + [(j, i) for i, j in pairs]


X_GROUPS = [[NX * z + x for x in range(NX)] for z in range(NZ)]
FAR_GROUPS = [[NX * (NL * h + l) + x for h in range(NL)] for l in range(NL) for x in range(NX)]


def near_groups(count_y):
    groups = []
    for y in range(count_y):
        for h in range(NL):
            for x in range(NX):
                z = [NL * h + l + (NL if y % 2 and l < NL // 2 else 0) for l in range(NL)]
                groups.append([(NX * (place % NZ) + x) * count_y + y for place in z])
    return groups


def exchange(value, groups):
    return lax.all_to_all(value, "gx", 0, 0, axis_index_groups=groups, tiled=True)


def body(blocks_a, prolong, aggregate, coupling_slot):
    count_x = lax.axis_size("gx")
    count_y = lax.axis_size("gy")
    own = prolong.reshape(E, B * B)
    ya = lax.ppermute(own, "gy", swaps(count_y, 0))
    yb = lax.ppermute(own, "gy", swaps(count_y, 1))
    xa = lax.ppermute(own, "gx", swaps(count_x, 0))
    xb = lax.ppermute(own, "gx", swaps(count_x, 1))
    matrix_a = blocks_a.reshape(E, K, B * B).transpose(1, 0, 2)
    slots = coupling_slot.transpose(2, 0, 1)
    c = exchange(products(aggregate, slots, matrix_a, own, xa, xb, ya, yb), X_GROUPS)
    t = lax.all_to_all(
        table(c), ("gx", "gy"), 0, 0, axis_index_groups=near_groups(count_y), tiled=True
    )
    return finish(exchange(partial_sums(t), FAR_GROUPS)).reshape(1, 1, CS, B * B)


def solution(mesh):
    return jax.shard_map(
        body,
        mesh=mesh,
        in_specs=(
            P("gx", "gy", None, None),
            P("gx", "gy", None),
            P("gx", "gy"),
            P("gx", "gy", None),
        ),
        out_specs=P("gx", "gy", None, None),
        check_vma=False,
    )
```

```python
import jax
import jax.numpy as jnp
from jax import lax
from jax.experimental import pallas as pl
from jax.experimental.pallas import tpu as pltpu
from jax.sharding import PartitionSpec as P

B = 64
K = 5
CS = 8
E = 8
Q = 32
LANES = 128
NX = 4
NZ = 16
NJ = NZ // 2
TEAM = 2 * NX


F32 = jnp.float32
BF16 = jnp.bfloat16


VMEM = pl.BlockSpec(memory_space=pltpu.VMEM)
SMEM = pl.BlockSpec(memory_space=pltpu.SMEM)


PARAMS = pltpu.CompilerParams(vmem_limit_bytes=24 * 1024 * 1024)


def near(value):
    return pltpu.with_memory_space_constraint(value, pltpu.VMEM)


def low_half(shape):
    return lax.broadcasted_iota(jnp.int32, shape, len(shape) - 1) < B


def two_rows(x, low):
    r = pltpu.roll(x, B, 1)
    return jnp.where(low, x, r), jnp.where(low, r, x)


def product(a2_ref, users, twice):
    low64 = low_half((B, LANES))
    zero = jnp.zeros_like(twice)
    weights = jnp.concatenate(
        [jnp.where(low64, twice, zero), jnp.where(low64, zero, twice)], axis=0
    ).astype(BF16)
    rows = [a2_ref[(k * E + e) * Q : (k * E + e + 1) * Q, :] for e, k in users]
    left = (rows[0] if len(rows) == 1 else jnp.concatenate(rows, axis=0)).astype(BF16)
    return jnp.dot(left, weights, preferred_element_type=F32).astype(BF16)


def own_kernel(agg_ref, slot_ref, a_ref, p_ref, a2, p2, t2, tags_ref, wd):
    lane = lax.broadcasted_iota(jnp.int32, (E, LANES), 1)
    tags = jnp.zeros((E, LANES), jnp.int32)
    for e in range(E):
        tags = jnp.where(lane == e, agg_ref[0, e], tags)
        for k in range(K):
            tags = jnp.where(lane == E + k * E + e, slot_ref[k, 0, e], tags)
    tags = jnp.concatenate([tags.astype(F32)] * (Q // E), axis=0).astype(BF16)
    tags_ref[...] = tags
    low8 = low_half((E, LANES))
    for k in range(K):
        for q in range(Q):
            x = a_ref[k, :, LANES * q : LANES * (q + 1)].astype(F32)
            a2[pl.ds(k * E * Q + q, E, stride=Q), :] = x
    for q in range(Q):
        x = p_ref[:, LANES * q : LANES * (q + 1)].astype(F32)
        p2[pl.ds(q, E, stride=Q), :] = x
        even, odd = two_rows(x, low8)
        wd[pl.ds(2 * q, E, stride=B), :] = even
        wd[pl.ds(2 * q + 1, E, stride=B), :] = odd
    for e in range(E):
        users = [(e, 0)]
        if e + 1 < E:
            users.append((e + 1, 3))
        if e > 0:
            users.append((e - 1, 4))
        result = product(a2, users, wd[e * B : (e + 1) * B, :])
        for place, (user, k) in enumerate(users):
            t2[user, :, LANES * k : LANES * (k + 1)] = result[place * Q : (place + 1) * Q]


def own_products(agg, slot, a, p):
    return pl.pallas_call(
        own_kernel,
        out_shape=(
            pltpu.VMEM((K * E * Q, LANES), F32),
            pltpu.VMEM((E * Q, LANES), F32),
            pltpu.VMEM((E, Q, K * LANES), BF16),
            pltpu.VMEM((Q, LANES), BF16),
        ),
        in_specs=[SMEM] * 2 + [VMEM] * 2,
        out_specs=(VMEM,) * 4,
        scratch_shapes=[pltpu.VMEM((E * B, LANES), F32)],
        compiler_params=PARAMS,
        name="own_products",
    )(agg, slot, a, p)


def beside_kernel(a2, p2, t2, tags, xa, xb, ya, yb, out_ref, wd):
    low8 = low_half((E, LANES))
    for number, ref in enumerate((xa, xb, ya, yb)):
        for q in range(Q):
            even, odd = two_rows(ref[:, LANES * q : LANES * (q + 1)].astype(F32), low8)
            base = number * E * B
            wd[pl.ds(base + 2 * q, E, stride=B), :] = even
            wd[pl.ds(base + 2 * q + 1, E, stride=B), :] = odd
    odd_x = lax.axis_index("gx") & 1
    odd_y = lax.axis_index("gy") & 1

    def multiply(number, e, k):
        return product(a2, [(e, k)], wd[pl.ds(pl.multiple_of(number * B, B), B), :])

    low32 = low_half((Q, LANES))
    for e in range(E):
        parts = [t2[e, :, LANES * k : LANES * (k + 1)] for k in range(K)]
        parts[1] = multiply(E - odd_x * E + e, e, 1)
        parts[2] = multiply(odd_x * E + e, e, 2)
        if e == 0:
            parts[3] = multiply(3 * E - odd_y * E + E - 1, e, 3)
        if e == E - 1:
            parts[4] = multiply(2 * E + odd_y * E, e, 4)
        pt = jnp.transpose(p2[e * Q : (e + 1) * Q, :]).astype(BF16)
        g = jnp.dot(pt, jnp.concatenate(parts, axis=1), preferred_element_type=F32)
        for k in range(K):
            u = g[:B, LANES * k : LANES * (k + 1)]
            v = g[B:, LANES * k : LANES * (k + 1)]
            first = u[:Q] + pltpu.roll(v[:Q], B, 1)
            second = pltpu.roll(u[Q:], B, 1) + v[Q:]
            block = jnp.where(low32, first, second).astype(BF16)
            for d in range(TEAM):
                out_ref[d, e * K + k] = block
    for d in range(TEAM):
        out_ref[d, E * K] = tags[...]


def contributions(own, beside):
    return pl.pallas_call(
        beside_kernel,
        out_shape=pltpu.VMEM((TEAM, E * K + 1, Q, LANES), BF16),
        in_specs=[VMEM] * 8,
        out_specs=VMEM,
        scratch_shapes=[pltpu.VMEM((4 * E * B, LANES), F32)],
        compiler_params=PARAMS,
        name="contributions",
    )(*map(near, own), *map(near, beside))


def table_kernel(c_ref, out_ref, tab, tags, scalars, sem):
    for source in range(TEAM):
        row = c_ref[source, E * K, :E].astype(F32).astype(jnp.int32)
        tags[source : source + 1, :] = row[:1]
    copy = pltpu.make_async_copy(tags, scalars, sem)
    copy.start()
    for block in range(NJ * CS):
        tab[block] = jnp.zeros((Q, LANES), F32)
    copy.wait()
    place = lax.axis_index("gx") & (2 * NX - 1)
    for source in range(TEAM):

        def take(e, carry, source=source):
            owner = scalars[source, e]

            @pl.when((owner & (2 * NX - 1)) == place)
            def _():
                base = (owner >> 3) * CS
                for k in range(K):
                    row = base + scalars[source, E + k * E + e]
                    tab[row] += c_ref[source, e * K + k].astype(F32)

            return carry

        lax.fori_loop(0, E, take, 0)
    for block in range(NJ * CS):
        out_ref[block // CS, block % CS] = tab[block].astype(BF16)


def table(c):
    return pl.pallas_call(
        table_kernel,
        out_shape=pltpu.VMEM((NJ, CS, Q, LANES), BF16),
        in_specs=[VMEM],
        out_specs=VMEM,
        scratch_shapes=[
            pltpu.VMEM((NJ * CS, Q, LANES), F32),
            pltpu.VMEM((TEAM, LANES), jnp.int32),
            pltpu.SMEM((TEAM, LANES), jnp.int32),
            pltpu.SemaphoreType.DMA,
        ],
        compiler_params=PARAMS,
        name="table",
    )(near(c))


def finish_kernel(r_ref, out_ref, total):
    for slot in range(CS):
        row = r_ref[0, slot].astype(F32)
        for source in range(1, NJ):
            row += r_ref[source, slot].astype(F32)
        total[slot * Q : (slot + 1) * Q, :] = row
    low8 = low_half((CS, LANES))
    for pair in range(Q // 2):
        even = total[pl.ds(2 * pair, CS, stride=Q), :]
        odd = total[pl.ds(2 * pair + 1, CS, stride=Q), :]
        out_ref[:, LANES * pair : LANES * (pair + 1)] = jnp.where(low8, even, pltpu.roll(odd, B, 1))
        place = pair + Q // 2
        out_ref[:, LANES * place : LANES * (place + 1)] = jnp.where(
            low8, pltpu.roll(even, B, 1), odd
        )


def finish(r):
    return pl.pallas_call(
        finish_kernel,
        out_shape=jax.ShapeDtypeStruct((CS, B * B), F32),
        in_specs=[VMEM],
        out_specs=VMEM,
        scratch_shapes=[pltpu.VMEM((CS * Q, LANES), F32)],
        compiler_params=PARAMS,
        name="finish",
    )(near(r))


def swaps(count, first):
    pairs = [(i, i + 1) for i in range(first, count - 1, 2)]
    return pairs + [(j, i) for i, j in pairs]


def teams(count_y):
    groups = []
    for y in range(count_y):
        for pair in range(NJ):
            places = [(2 * pair + y % 2 + side) % NZ for side in range(2)]
            groups.append([(NX * z + x) * count_y + y for z in places for x in range(NX)])
    return groups


CLASSES = [[NX * (2 * j + parity) + x for j in range(NJ)] for parity in range(2) for x in range(NX)]


def body(blocks_a, prolong, aggregate, coupling_slot):
    count_x = lax.axis_size("gx")
    count_y = lax.axis_size("gy")
    p = prolong.reshape(E, B * B)
    ya = lax.ppermute(p, "gy", swaps(count_y, 0))
    yb = lax.ppermute(p, "gy", swaps(count_y, 1))
    xa = lax.ppermute(p, "gx", swaps(count_x, 0))
    xb = lax.ppermute(p, "gx", swaps(count_x, 1))
    slots = coupling_slot.transpose(2, 0, 1)
    own = own_products(aggregate, slots, blocks_a.reshape(E, K, B * B).transpose(1, 0, 2), p)
    c = contributions(own, (xa, xb, ya, yb))
    c = lax.all_to_all(c, ("gx", "gy"), 0, 0, axis_index_groups=teams(count_y), tiled=True)
    r = lax.all_to_all(table(c), "gx", 0, 0, axis_index_groups=CLASSES, tiled=True)
    return finish(r).reshape(1, 1, CS, B * B)


def solution(mesh):
    return jax.shard_map(
        body,
        mesh=mesh,
        in_specs=(
            P("gx", "gy", None, None),
            P("gx", "gy", None),
            P("gx", "gy"),
            P("gx", "gy", None),
        ),
        out_specs=P("gx", "gy", None, None),
        check_vma=False,
    )
```

```python
import jax
import jax.numpy as jnp
from jax import lax
from jax.experimental import pallas as pl
from jax.experimental.pallas import tpu as pltpu
from jax.sharding import PartitionSpec as P

B = 64
K = 5
CS = 8
E = 8
Q = 32
LANES = 128
NX = 4
NZ = 16
NL = 4
TEAM = NX * NL
ROWS = E * K + E


F32 = jnp.float32
BF16 = jnp.bfloat16


VMEM = pl.BlockSpec(memory_space=pltpu.VMEM)
SMEM = pl.BlockSpec(memory_space=pltpu.SMEM)


PARAMS = pltpu.CompilerParams(vmem_limit_bytes=24 * 1024 * 1024)


def near(value):
    return pltpu.with_memory_space_constraint(value, pltpu.VMEM)


def low_half(shape):
    return lax.broadcasted_iota(jnp.int32, shape, len(shape) - 1) < B


def two_rows(x, low):
    r = pltpu.roll(x, B, 1)
    return jnp.where(low, x, r), jnp.where(low, r, x)


def product(a2_ref, users, twice):
    low64 = low_half((B, LANES))
    zero = jnp.zeros_like(twice)
    weights = jnp.concatenate(
        [jnp.where(low64, twice, zero), jnp.where(low64, zero, twice)], axis=0
    ).astype(BF16)
    rows = [a2_ref[(k * E + e) * Q : (k * E + e + 1) * Q, :] for e, k in users]
    left = (rows[0] if len(rows) == 1 else jnp.concatenate(rows, axis=0)).astype(BF16)
    return jnp.dot(left, weights, preferred_element_type=F32).astype(BF16)


def own_kernel(agg_ref, slot_ref, a_ref, p_ref, a2, p2, t2, tags_ref, wd):
    place = lax.broadcasted_iota(jnp.int32, (E, LANES), 0) * LANES
    place += lax.broadcasted_iota(jnp.int32, (E, LANES), 1)
    place -= (lax.axis_index("gx") & (TEAM - 1)) * ROWS
    owner = jnp.zeros((E, LANES), jnp.int32)
    slot = jnp.zeros((E, LANES), jnp.int32)
    for e in range(E):
        for k in range(K):
            here = place == e * K + k
            owner = jnp.where(here, agg_ref[0, e], owner)
            slot = jnp.where(here, slot_ref[k, 0, e], slot)
    team = (((owner >> 2) - 2 * (lax.axis_index("gy") & 1)) & (NZ - 1)) >> 2
    owner = team * TEAM + (owner & (TEAM - 1))
    inside = (place >= 0) & (place < E * K)
    none = (place >= E * K) & (place < ROWS)
    owner = jnp.where(inside, owner, jnp.where(none, NZ * NX, 0))
    tags_ref[0] = owner.astype(F32)
    tags_ref[1] = slot.astype(F32)
    low8 = low_half((E, LANES))
    for k in range(K):
        for q in range(Q):
            x = a_ref[k, :, LANES * q : LANES * (q + 1)].astype(F32)
            a2[pl.ds(k * E * Q + q, E, stride=Q), :] = x
    for q in range(Q):
        x = p_ref[:, LANES * q : LANES * (q + 1)].astype(F32)
        p2[pl.ds(q, E, stride=Q), :] = x
        even, odd = two_rows(x, low8)
        wd[pl.ds(2 * q, E, stride=B), :] = even
        wd[pl.ds(2 * q + 1, E, stride=B), :] = odd
    for e in range(E):
        users = [(e, 0)]
        if e + 1 < E:
            users.append((e + 1, 3))
        if e > 0:
            users.append((e - 1, 4))
        result = product(a2, users, wd[e * B : (e + 1) * B, :])
        for place, (user, k) in enumerate(users):
            t2[user, :, LANES * k : LANES * (k + 1)] = result[place * Q : (place + 1) * Q]


def own_products(agg, slot, a, p):
    return pl.pallas_call(
        own_kernel,
        out_shape=(
            pltpu.VMEM((K * E * Q, LANES), F32),
            pltpu.VMEM((E * Q, LANES), F32),
            pltpu.VMEM((E, Q, K * LANES), BF16),
            pltpu.VMEM((2, E, LANES), F32),
        ),
        in_specs=[SMEM] * 2 + [VMEM] * 2,
        out_specs=(VMEM,) * 4,
        scratch_shapes=[pltpu.VMEM((E * B, LANES), F32)],
        compiler_params=PARAMS,
        name="own_products",
    )(agg, slot, a, p)


def beside_kernel(a2, p2, t2, tags, xa, xb, ya, yb, out_ref, wd, sums):
    low8 = low_half((E, LANES))
    for number, ref in enumerate((xa, xb, ya, yb)):
        for q in range(Q):
            even, odd = two_rows(ref[:, LANES * q : LANES * (q + 1)].astype(F32), low8)
            base = number * E * B
            wd[pl.ds(base + 2 * q, E, stride=B), :] = even
            wd[pl.ds(base + 2 * q + 1, E, stride=B), :] = odd
    odd_x = lax.axis_index("gx") & 1
    odd_y = lax.axis_index("gy") & 1

    def multiply(number, e, k):
        return product(a2, [(e, k)], wd[pl.ds(pl.multiple_of(number * B, B), B), :])

    low32 = low_half((Q, LANES))
    for e in range(E):
        parts = [t2[e, :, LANES * k : LANES * (k + 1)] for k in range(K)]
        parts[1] = multiply(E - odd_x * E + e, e, 1)
        parts[2] = multiply(odd_x * E + e, e, 2)
        if e == 0:
            parts[3] = multiply(3 * E - odd_y * E + E - 1, e, 3)
        if e == E - 1:
            parts[4] = multiply(2 * E + odd_y * E, e, 4)
        pt = jnp.transpose(p2[e * Q : (e + 1) * Q, :]).astype(BF16)
        g = jnp.dot(pt, jnp.concatenate(parts, axis=1), preferred_element_type=F32)
        for k in range(K):
            u = g[:B, LANES * k : LANES * (k + 1)]
            v = g[B:, LANES * k : LANES * (k + 1)]
            first = u[:Q] + pltpu.roll(v[:Q], B, 1)
            second = pltpu.roll(u[Q:], B, 1) + v[Q:]
            row = e * K + k
            sums[row * Q : (row + 1) * Q, :] = jnp.where(low32, first, second)
    for b in range(Q):
        rows = [sums[pl.ds(e * E * Q + b, E, stride=Q), :] for e in range(K)]
        rows.append(tags[b % 2])
        out_ref[b // 2, b % 2] = jnp.concatenate(rows, axis=0).astype(BF16)


def contributions(own, beside):
    return pl.pallas_call(
        beside_kernel,
        out_shape=pltpu.VMEM((TEAM, 2, ROWS, LANES), BF16),
        in_specs=[VMEM] * 8,
        out_specs=VMEM,
        scratch_shapes=[
            pltpu.VMEM((4 * E * B, LANES), F32),
            pltpu.VMEM((E * K * Q, LANES), F32),
        ],
        compiler_params=PARAMS,
        name="contributions",
    )(*map(near, own), *map(near, beside))


def table_kernel(c_ref, out_ref):
    owner = c_ref[0, 0, E * K :].astype(F32)
    slot = c_ref[0, 1, E * K :].astype(F32)
    for source in range(1, TEAM):
        owner += c_ref[source, 0, E * K :].astype(F32)
        slot += c_ref[source, 1, E * K :].astype(F32)
    code = (owner * CS + slot).astype(jnp.int32)
    halves = [c_ref[:, t].reshape(TEAM * ROWS, LANES) for t in range(2)]
    rows = jnp.concatenate(halves, axis=1)
    target = lax.broadcasted_iota(jnp.int32, (TEAM * CS, LANES), 0)
    for far in range(NL):
        chosen = [
            (target + far * TEAM * CS == code[i : i + 1]).astype(F32).astype(BF16)
            for i in range(TEAM * ROWS // LANES)
        ]
        total = jnp.dot(jnp.concatenate(chosen, axis=1), rows, preferred_element_type=F32)
        out_ref[far] = total.astype(BF16)


def table(c):
    return pl.pallas_call(
        table_kernel,
        out_shape=pltpu.VMEM((NL, TEAM * CS, 2 * LANES), BF16),
        in_specs=[VMEM],
        out_specs=VMEM,
        compiler_params=PARAMS,
        name="table",
    )(near(c))


def total_kernel(t_ref, out_ref):
    for place in range(TEAM):
        rows = slice(place * CS, (place + 1) * CS)
        total = t_ref[0, rows].astype(F32)
        for source in range(1, NL):
            total += t_ref[source, rows].astype(F32)
        out_ref[place] = total


def totals(t):
    return pl.pallas_call(
        total_kernel,
        out_shape=pltpu.VMEM((TEAM, CS, 2 * LANES), F32),
        in_specs=[VMEM],
        out_specs=VMEM,
        compiler_params=PARAMS,
        name="totals",
    )(near(t))


def finish_kernel(r_ref, out_ref):
    low8 = low_half((CS, LANES))
    for pair in range(Q // 2):
        even = r_ref[pair, :, :LANES]
        odd = r_ref[pair, :, LANES:]
        out_ref[:, LANES * pair : LANES * (pair + 1)] = jnp.where(low8, even, pltpu.roll(odd, B, 1))
        place = pair + Q // 2
        out_ref[:, LANES * place : LANES * (place + 1)] = jnp.where(
            low8, pltpu.roll(even, B, 1), odd
        )


def finish(r):
    return pl.pallas_call(
        finish_kernel,
        out_shape=jax.ShapeDtypeStruct((CS, B * B), F32),
        in_specs=[VMEM],
        out_specs=VMEM,
        compiler_params=PARAMS,
        name="finish",
    )(near(r))


def swaps(count, first):
    pairs = [(i, i + 1) for i in range(first, count - 1, 2)]
    return pairs + [(j, i) for i, j in pairs]


def blocks_of_z(y, block):
    return [(NL * block + l + (NL if y % 2 and l < NL // 2 else 0)) % NZ for l in range(NL)]


def teams(count_y):
    return [
        [(NX * z + x) * count_y + y for z in blocks_of_z(y, block) for x in range(NX)]
        for y in range(count_y)
        for block in range(NL)
    ]


def far_groups(count_y):
    return [
        [(NX * blocks_of_z(y, block)[l] + x) * count_y + y for block in range(NL)]
        for y in range(count_y)
        for l in range(NL)
        for x in range(NX)
    ]


def exchange(value, groups):
    return lax.all_to_all(value, ("gx", "gy"), 0, 0, axis_index_groups=groups, tiled=True)


def body(blocks_a, prolong, aggregate, coupling_slot):
    count_x = lax.axis_size("gx")
    count_y = lax.axis_size("gy")
    p = prolong.reshape(E, B * B)
    ya = lax.ppermute(p, "gy", swaps(count_y, 0))
    yb = lax.ppermute(p, "gy", swaps(count_y, 1))
    xa = lax.ppermute(p, "gx", swaps(count_x, 0))
    xb = lax.ppermute(p, "gx", swaps(count_x, 1))
    slots = coupling_slot.transpose(2, 0, 1)
    own = own_products(aggregate, slots, blocks_a.reshape(E, K, B * B).transpose(1, 0, 2), p)
    c = contributions(own, (xa, xb, ya, yb))
    c = exchange(c, teams(count_y))
    t = exchange(table(c), far_groups(count_y))
    r = exchange(totals(t), teams(count_y))
    return finish(r).reshape(1, 1, CS, B * B)


def solution(mesh):
    return jax.shard_map(
        body,
        mesh=mesh,
        in_specs=(
            P("gx", "gy", None, None),
            P("gx", "gy", None),
            P("gx", "gy"),
            P("gx", "gy", None),
        ),
        out_specs=P("gx", "gy", None, None),
        check_vma=False,
    )
```

```python
import jax
import jax.numpy as jnp
from jax import lax
from jax.experimental import pallas as pl
from jax.experimental.pallas import tpu as pltpu
from jax.sharding import PartitionSpec as P

B = 64
K = 5
CS = 8
E = 8
Q = 32
LANES = 128
NX = 4
NZ = 16
NL = 4
TEAM = NX * NL
ROWS = E * K + E


F32 = jnp.float32
BF16 = jnp.bfloat16


VMEM = pl.BlockSpec(memory_space=pltpu.VMEM)
SMEM = pl.BlockSpec(memory_space=pltpu.SMEM)


PARAMS = pltpu.CompilerParams(vmem_limit_bytes=24 * 1024 * 1024)


def near(value):
    return pltpu.with_memory_space_constraint(value, pltpu.VMEM)


def low_half(shape):
    return lax.broadcasted_iota(jnp.int32, shape, len(shape) - 1) < B


def two_rows(x, low):
    r = pltpu.roll(x, B, 1)
    return jnp.where(low, x, r), jnp.where(low, r, x)


def product(a2_ref, users, twice):
    low64 = low_half((B, LANES))
    zero = jnp.zeros_like(twice)
    weights = jnp.concatenate(
        [jnp.where(low64, twice, zero), jnp.where(low64, zero, twice)], axis=0
    ).astype(BF16)
    rows = [a2_ref[(k * E + e) * Q : (k * E + e + 1) * Q, :] for e, k in users]
    left = (rows[0] if len(rows) == 1 else jnp.concatenate(rows, axis=0)).astype(BF16)
    return jnp.dot(left, weights, preferred_element_type=F32).astype(BF16)


def own_kernel(
    agg_hbm, slot_hbm, a_hbm, p_hbm, a2, p2, t2, tags_ref, wd, a_ref, p_ref, agg_ref, slot_ref, sems
):
    pairs = ((agg_hbm, agg_ref), (slot_hbm, slot_ref), (p_hbm, p_ref), (a_hbm, a_ref))
    copies = [pltpu.make_async_copy(*pair, sems.at[i]) for i, pair in enumerate(pairs)]
    for copy in copies:
        copy.start()
    copies[0].wait()
    copies[1].wait()
    place = lax.broadcasted_iota(jnp.int32, (E, LANES), 0) * LANES
    place += lax.broadcasted_iota(jnp.int32, (E, LANES), 1)
    place -= (lax.axis_index("gx") & (TEAM - 1)) * ROWS
    owner = jnp.zeros((E, LANES), jnp.int32)
    slot = jnp.zeros((E, LANES), jnp.int32)
    for e in range(E):
        for k in range(K):
            here = place == e * K + k
            owner = jnp.where(here, agg_ref[0, e], owner)
            slot = jnp.where(here, slot_ref[k, 0, e], slot)
    inside = (place >= 0) & (place < E * K)
    none = (place >= E * K) & (place < ROWS)
    owner = jnp.where(inside, owner, jnp.where(none, NZ * NX, 0))
    tags_ref[0] = owner.astype(F32)
    tags_ref[1] = slot.astype(F32)
    low8 = low_half((E, LANES))
    copies[2].wait()
    for q in range(Q):
        x = p_ref[:, LANES * q : LANES * (q + 1)].astype(F32)
        p2[pl.ds(q, E, stride=Q), :] = x
        even, odd = two_rows(x, low8)
        wd[pl.ds(2 * q, E, stride=B), :] = even
        wd[pl.ds(2 * q + 1, E, stride=B), :] = odd
    copies[3].wait()
    for k in range(K):
        for q in range(Q):
            x = a_ref[k, :, LANES * q : LANES * (q + 1)].astype(F32)
            a2[pl.ds(k * E * Q + q, E, stride=Q), :] = x
    for e in range(E):
        users = [(e, 0)]
        if e + 1 < E:
            users.append((e + 1, 3))
        if e > 0:
            users.append((e - 1, 4))
        result = product(a2, users, wd[e * B : (e + 1) * B, :])
        for place, (user, k) in enumerate(users):
            t2[user, :, LANES * k : LANES * (k + 1)] = result[place * Q : (place + 1) * Q]


def own_products(agg, slot, a, p):
    return pl.pallas_call(
        own_kernel,
        out_shape=(
            pltpu.VMEM((K * E * Q, LANES), F32),
            pltpu.VMEM((E * Q, LANES), F32),
            pltpu.VMEM((E, Q, K * LANES), BF16),
            pltpu.VMEM((2, E, LANES), F32),
        ),
        in_specs=[pl.BlockSpec(memory_space=pltpu.HBM)] * 4,
        out_specs=(VMEM,) * 4,
        scratch_shapes=[
            pltpu.VMEM((E * B, LANES), F32),
            pltpu.VMEM((K, E, B * B), BF16),
            pltpu.VMEM((E, B * B), BF16),
            pltpu.SMEM((1, E), jnp.int32),
            pltpu.SMEM((K, 1, E), jnp.int32),
            pltpu.SemaphoreType.DMA((4,)),
        ],
        compiler_params=PARAMS,
        name="own_products",
    )(*(pltpu.with_memory_space_constraint(v, pltpu.HBM) for v in (agg, slot, a, p)))


def beside_kernel(a2, p2, t2, tags, xa, xb, ya, yb, out_ref, wd, sums):
    low8 = low_half((E, LANES))
    for number, ref in enumerate((xa, xb, ya, yb)):
        for q in range(Q):
            even, odd = two_rows(ref[:, LANES * q : LANES * (q + 1)].astype(F32), low8)
            base = number * E * B
            wd[pl.ds(base + 2 * q, E, stride=B), :] = even
            wd[pl.ds(base + 2 * q + 1, E, stride=B), :] = odd
    odd_x = lax.axis_index("gx") & 1
    odd_y = lax.axis_index("gy") & 1

    def multiply(number, e, k):
        return product(a2, [(e, k)], wd[pl.ds(pl.multiple_of(number * B, B), B), :])

    low32 = low_half((Q, LANES))
    for e in range(E):
        parts = [t2[e, :, LANES * k : LANES * (k + 1)] for k in range(K)]
        parts[1] = multiply(E - odd_x * E + e, e, 1)
        parts[2] = multiply(odd_x * E + e, e, 2)
        if e == 0:
            parts[3] = multiply(3 * E - odd_y * E + E - 1, e, 3)
        if e == E - 1:
            parts[4] = multiply(2 * E + odd_y * E, e, 4)
        pt = jnp.transpose(p2[e * Q : (e + 1) * Q, :]).astype(BF16)
        g = jnp.dot(pt, jnp.concatenate(parts, axis=1), preferred_element_type=F32)
        for k in range(K):
            u = g[:B, LANES * k : LANES * (k + 1)]
            v = g[B:, LANES * k : LANES * (k + 1)]
            first = u[:Q] + pltpu.roll(v[:Q], B, 1)
            second = pltpu.roll(u[Q:], B, 1) + v[Q:]
            row = e * K + k
            sums[row * Q : (row + 1) * Q, :] = jnp.where(low32, first, second)
    for b in range(Q):
        rows = [sums[pl.ds(e * E * Q + b, E, stride=Q), :] for e in range(K)]
        rows.append(tags[b % 2])
        out_ref[b // 2, b % 2] = jnp.concatenate(rows, axis=0).astype(BF16)


def contributions(own, beside):
    return pl.pallas_call(
        beside_kernel,
        out_shape=pltpu.VMEM((TEAM, 2, ROWS, LANES), BF16),
        in_specs=[VMEM] * 8,
        out_specs=VMEM,
        scratch_shapes=[
            pltpu.VMEM((4 * E * B, LANES), F32),
            pltpu.VMEM((E * K * Q, LANES), F32),
        ],
        compiler_params=PARAMS,
        name="contributions",
    )(*map(near, own), *map(near, beside))


def table_kernel(c_ref, out_ref):
    owner = c_ref[0, 0, E * K :].astype(F32)
    slot = c_ref[0, 1, E * K :].astype(F32)
    for source in range(1, TEAM):
        owner += c_ref[source, 0, E * K :].astype(F32)
        slot += c_ref[source, 1, E * K :].astype(F32)
    code = (owner * CS + slot).astype(jnp.int32)
    halves = [c_ref[:, t].reshape(TEAM * ROWS, LANES) for t in range(2)]
    rows = jnp.concatenate(halves, axis=1)
    target = lax.broadcasted_iota(jnp.int32, (TEAM * CS, LANES), 0)
    for far in range(NL):
        chosen = [
            (target + far * TEAM * CS == code[i : i + 1]).astype(F32).astype(BF16)
            for i in range(TEAM * ROWS // LANES)
        ]
        total = jnp.dot(jnp.concatenate(chosen, axis=1), rows, preferred_element_type=F32)
        out_ref[far * TEAM : (far + 1) * TEAM] = total.reshape(TEAM, CS, 2 * LANES).astype(BF16)


def table(c):
    return pl.pallas_call(
        table_kernel,
        out_shape=pltpu.VMEM((NL * TEAM, CS, 2 * LANES), BF16),
        in_specs=[VMEM],
        out_specs=VMEM,
        compiler_params=PARAMS,
        name="table",
    )(near(c))


def finish_kernel(r_ref, out_ref):
    low8 = low_half((CS, LANES))
    for pair in range(Q // 2):
        part = r_ref[pair].astype(F32)
        for far in range(1, NL):
            part += r_ref[far * TEAM + pair].astype(F32)
        even = part[:, :LANES]
        odd = part[:, LANES:]
        out_ref[:, LANES * pair : LANES * (pair + 1)] = jnp.where(low8, even, pltpu.roll(odd, B, 1))
        place = pair + Q // 2
        out_ref[:, LANES * place : LANES * (place + 1)] = jnp.where(
            low8, pltpu.roll(even, B, 1), odd
        )


def finish(r):
    return pl.pallas_call(
        finish_kernel,
        out_shape=jax.ShapeDtypeStruct((CS, B * B), F32),
        in_specs=[VMEM],
        out_specs=VMEM,
        compiler_params=PARAMS,
        name="finish",
    )(near(r))


def swaps(count, first):
    pairs = [(i, i + 1) for i in range(first, count - 1, 2)]
    return pairs + [(j, i) for i, j in pairs]


def blocks_of_z(y, block):
    return [(NL * block + l + (NL if y % 2 and l < NL // 2 else 0)) % NZ for l in range(NL)]


def teams(count_y):
    return [
        [(NX * z + x) * count_y + y for z in blocks_of_z(y, block) for x in range(NX)]
        for y in range(count_y)
        for block in range(NL)
    ]


def body(blocks_a, prolong, aggregate, coupling_slot):
    count_x = lax.axis_size("gx")
    count_y = lax.axis_size("gy")
    p = prolong.reshape(E, B * B)
    ya = lax.ppermute(p, "gy", swaps(count_y, 0))
    yb = lax.ppermute(p, "gy", swaps(count_y, 1))
    xa = lax.ppermute(p, "gx", swaps(count_x, 0))
    xb = lax.ppermute(p, "gx", swaps(count_x, 1))
    slots = coupling_slot.transpose(2, 0, 1)
    own = own_products(aggregate, slots, blocks_a.reshape(E, K, B * B).transpose(1, 0, 2), p)
    c = contributions(own, (xa, xb, ya, yb))
    c = lax.all_to_all(c, ("gx", "gy"), 0, 0, axis_index_groups=teams(count_y), tiled=True)
    r = lax.all_to_all(table(c), "gx", 0, 0, tiled=True)
    return finish(r).reshape(1, 1, CS, B * B)


def solution(mesh):
    return jax.shard_map(
        body,
        mesh=mesh,
        in_specs=(
            P("gx", "gy", None, None),
            P("gx", "gy", None),
            P("gx", "gy"),
            P("gx", "gy", None),
        ),
        out_specs=P("gx", "gy", None, None),
        check_vma=False,
    )
```

```python
import jax
import jax.numpy as jnp
from jax import lax
from jax.experimental import pallas as pl
from jax.experimental.pallas import tpu as pltpu
from jax.sharding import PartitionSpec as P

B = 64
K = 5
CS = 8
E = 8
Q = 32
LANES = 128
NX = 4
NZ = 16
NL = 4
TEAM = NX * NL
ROWS = E * K + E


F32 = jnp.float32
BF16 = jnp.bfloat16


VMEM = pl.BlockSpec(memory_space=pltpu.VMEM)
SMEM = pl.BlockSpec(memory_space=pltpu.SMEM)


PARAMS = pltpu.CompilerParams(vmem_limit_bytes=24 * 1024 * 1024)


def near(value):
    return pltpu.with_memory_space_constraint(value, pltpu.VMEM)


def low_half(shape):
    return lax.broadcasted_iota(jnp.int32, shape, len(shape) - 1) < B


def two_rows(x, low):
    r = pltpu.roll(x, B, 1)
    return jnp.where(low, x, r), jnp.where(low, r, x)


def product(a2_ref, users, twice):
    low64 = low_half((B, LANES))
    zero = jnp.zeros_like(twice)
    weights = jnp.concatenate(
        [jnp.where(low64, twice, zero), jnp.where(low64, zero, twice)], axis=0
    ).astype(BF16)
    rows = [a2_ref[pl.ds(k * E * Q + e, Q, stride=E), :] for e, k in users]
    left = (rows[0] if len(rows) == 1 else jnp.concatenate(rows, axis=0)).astype(BF16)
    return jnp.dot(left, weights, preferred_element_type=F32).astype(BF16)


def own_kernel(
    agg_hbm, slot_hbm, a_hbm, p_hbm, a2, p2, t2, tags_ref, wd, a_ref, p_ref, agg_ref, slot_ref, sems
):
    pairs = ((agg_hbm, agg_ref), (slot_hbm, slot_ref), (p_hbm, p_ref), (a_hbm, a_ref))
    copies = [pltpu.make_async_copy(*pair, sems.at[i]) for i, pair in enumerate(pairs)]
    for copy in copies:
        copy.start()
    copies[0].wait()
    copies[1].wait()
    place = lax.broadcasted_iota(jnp.int32, (E, LANES), 0) * LANES
    place += lax.broadcasted_iota(jnp.int32, (E, LANES), 1)
    place -= (lax.axis_index("gx") & (TEAM - 1)) * ROWS
    owner = jnp.zeros((E, LANES), jnp.int32)
    slot = jnp.zeros((E, LANES), jnp.int32)
    for e in range(E):
        for k in range(K):
            here = place == e * K + k
            owner = jnp.where(here, agg_ref[0, e], owner)
            slot = jnp.where(here, slot_ref[k, 0, e], slot)
    inside = (place >= 0) & (place < E * K)
    none = (place >= E * K) & (place < ROWS)
    owner = jnp.where(inside, owner, jnp.where(none, NZ * NX, 0))
    tags_ref[0] = owner.astype(F32)
    tags_ref[1] = slot.astype(F32)
    low8 = low_half((E, LANES))
    copies[2].wait()
    for q in range(Q):
        x = p_ref[:, LANES * q : LANES * (q + 1)].astype(F32)
        p2[E * q : E * (q + 1), :] = x
        even, odd = two_rows(x, low8)
        wd[2 * E * q : 2 * E * q + E, :] = even
        wd[2 * E * q + E : 2 * E * (q + 1), :] = odd
    copies[3].wait()
    for k in range(K):
        for q in range(Q):
            x = a_ref[k, :, LANES * q : LANES * (q + 1)].astype(F32)
            a2[(k * Q + q) * E : (k * Q + q + 1) * E, :] = x
    for e in range(E):
        users = [(e, 0)]
        if e + 1 < E:
            users.append((e + 1, 3))
        if e > 0:
            users.append((e - 1, 4))
        result = product(a2, users, wd[pl.ds(e, B, stride=E), :])
        for place, (user, k) in enumerate(users):
            t2[user, :, LANES * k : LANES * (k + 1)] = result[place * Q : (place + 1) * Q]


def own_products(agg, slot, a, p):
    return pl.pallas_call(
        own_kernel,
        out_shape=(
            pltpu.VMEM((K * E * Q, LANES), F32),
            pltpu.VMEM((E * Q, LANES), F32),
            pltpu.VMEM((E, Q, K * LANES), BF16),
            pltpu.VMEM((2, E, LANES), F32),
        ),
        in_specs=[pl.BlockSpec(memory_space=pltpu.HBM)] * 4,
        out_specs=(VMEM,) * 4,
        scratch_shapes=[
            pltpu.VMEM((E * B, LANES), F32),
            pltpu.VMEM((K, E, B * B), BF16),
            pltpu.VMEM((E, B * B), BF16),
            pltpu.SMEM((1, E), jnp.int32),
            pltpu.SMEM((K, 1, E), jnp.int32),
            pltpu.SemaphoreType.DMA((4,)),
        ],
        compiler_params=PARAMS,
        name="own_products",
    )(*(pltpu.with_memory_space_constraint(v, pltpu.HBM) for v in (agg, slot, a, p)))


def beside_kernel(a2, p2, t2, tags, ya, yb, xa, xb, out_ref, wd, sums):
    low8 = low_half((E, LANES))
    for number, ref in enumerate((xa, xb, ya, yb)):
        for q in range(Q):
            even, odd = two_rows(ref[:, LANES * q : LANES * (q + 1)].astype(F32), low8)
            base = number * E * B
            wd[base + 2 * E * q : base + 2 * E * q + E, :] = even
            wd[base + 2 * E * q + E : base + 2 * E * (q + 1), :] = odd
    odd_x = lax.axis_index("gx") & 1
    odd_y = lax.axis_index("gy") & 1

    def multiply(number, beside, e, k):
        start = pl.multiple_of(number * E * B, E) + beside
        return product(a2, [(e, k)], wd[pl.ds(start, B, stride=E), :])

    low32 = low_half((Q, LANES))
    for e in range(E):
        parts = [t2[e, :, LANES * k : LANES * (k + 1)] for k in range(K)]
        parts[1] = multiply(1 - odd_x, e, e, 1)
        parts[2] = multiply(odd_x, e, e, 2)
        if e == 0:
            parts[3] = multiply(3 - odd_y, E - 1, e, 3)
        if e == E - 1:
            parts[4] = multiply(2 + odd_y, 0, e, 4)
        pt = jnp.transpose(p2[pl.ds(e, Q, stride=E), :]).astype(BF16)
        g = jnp.dot(pt, jnp.concatenate(parts, axis=1), preferred_element_type=F32)
        for k in range(K):
            u = g[:B, LANES * k : LANES * (k + 1)]
            v = g[B:, LANES * k : LANES * (k + 1)]
            first = u[:Q] + pltpu.roll(v[:Q], B, 1)
            second = pltpu.roll(u[Q:], B, 1) + v[Q:]
            block = jnp.where(low32, first, second)
            for i in range(Q // E):
                start = (i * E * K + e * K + k) * E
                sums[start : start + E, :] = block[i * E : (i + 1) * E]
    for b in range(Q):
        starts = [(b // E * E * K + E * group) * E + b % E for group in range(K)]
        rows = [sums[pl.ds(start, E, stride=E), :] for start in starts]
        rows.append(tags[b % 2])
        out_ref[b // 2, b % 2] = jnp.concatenate(rows, axis=0).astype(BF16)


def contributions(own, beside):
    return pl.pallas_call(
        beside_kernel,
        out_shape=pltpu.VMEM((TEAM, 2, ROWS, LANES), BF16),
        in_specs=[VMEM] * 8,
        out_specs=VMEM,
        scratch_shapes=[
            pltpu.VMEM((4 * E * B, LANES), F32),
            pltpu.VMEM((E * K * Q, LANES), F32),
        ],
        compiler_params=PARAMS,
        name="contributions",
    )(*map(near, own), *map(near, beside))


def table_kernel(c_ref, out_ref):
    owner = c_ref[0, 0, E * K :].astype(F32)
    slot = c_ref[0, 1, E * K :].astype(F32)
    for source in range(1, TEAM):
        owner += c_ref[source, 0, E * K :].astype(F32)
        slot += c_ref[source, 1, E * K :].astype(F32)
    code = (owner * CS + slot).astype(jnp.int32)
    halves = [c_ref[:, t].reshape(TEAM * ROWS, LANES) for t in range(2)]
    rows = jnp.concatenate(halves, axis=1)
    target = lax.broadcasted_iota(jnp.int32, (TEAM * CS, LANES), 0)
    for far in range(NL):
        chosen = [
            (target + far * TEAM * CS == code[i : i + 1]).astype(F32).astype(BF16)
            for i in range(TEAM * ROWS // LANES)
        ]
        total = jnp.dot(jnp.concatenate(chosen, axis=1), rows, preferred_element_type=F32)
        out_ref[far * TEAM : (far + 1) * TEAM] = total.reshape(TEAM, CS, 2 * LANES).astype(BF16)


def table(c):
    return pl.pallas_call(
        table_kernel,
        out_shape=pltpu.VMEM((NL * TEAM, CS, 2 * LANES), BF16),
        in_specs=[VMEM],
        out_specs=VMEM,
        compiler_params=PARAMS,
        name="table",
    )(near(c))


def finish_kernel(r_ref, out_ref):
    low8 = low_half((CS, LANES))
    for pair in range(Q // 2):
        part = r_ref[pair].astype(F32)
        for far in range(1, NL):
            part += r_ref[far * TEAM + pair].astype(F32)
        even = part[:, :LANES]
        odd = part[:, LANES:]
        out_ref[:, LANES * pair : LANES * (pair + 1)] = jnp.where(low8, even, pltpu.roll(odd, B, 1))
        place = pair + Q // 2
        out_ref[:, LANES * place : LANES * (place + 1)] = jnp.where(
            low8, pltpu.roll(even, B, 1), odd
        )


def finish(r):
    return pl.pallas_call(
        finish_kernel,
        out_shape=jax.ShapeDtypeStruct((CS, B * B), F32),
        in_specs=[VMEM],
        out_specs=VMEM,
        compiler_params=PARAMS,
        name="finish",
    )(near(r))


def swaps(count, first):
    pairs = [(i, i + 1) for i in range(first, count - 1, 2)]
    return pairs + [(j, i) for i, j in pairs]


def blocks_of_z(y, block):
    return [(NL * block + l + (NL if y % 2 and l < NL // 2 else 0)) % NZ for l in range(NL)]


def teams(count_y):
    return [
        [(NX * z + x) * count_y + y for z in blocks_of_z(y, block) for x in range(NX)]
        for y in range(count_y)
        for block in range(NL)
    ]


def body(blocks_a, prolong, aggregate, coupling_slot):
    count_x = lax.axis_size("gx")
    count_y = lax.axis_size("gy")
    p = prolong.reshape(E, B * B)
    ya = lax.ppermute(p, "gy", swaps(count_y, 0))
    yb = lax.ppermute(p, "gy", swaps(count_y, 1))
    xa = lax.ppermute(p, "gx", swaps(count_x, 0))
    xb = lax.ppermute(p, "gx", swaps(count_x, 1))
    slots = coupling_slot.transpose(2, 0, 1)
    own = own_products(aggregate, slots, blocks_a.reshape(E, K, B * B).transpose(1, 0, 2), p)
    c = contributions(own, (ya, yb, xa, xb))
    c = lax.all_to_all(c, ("gx", "gy"), 0, 0, axis_index_groups=teams(count_y), tiled=True)
    r = lax.all_to_all(table(c), "gx", 0, 0, tiled=True)
    return finish(r).reshape(1, 1, CS, B * B)


def solution(mesh):
    return jax.shard_map(
        body,
        mesh=mesh,
        in_specs=(
            P("gx", "gy", None, None),
            P("gx", "gy", None),
            P("gx", "gy"),
            P("gx", "gy", None),
        ),
        out_specs=P("gx", "gy", None, None),
        check_vma=False,
    )
```

```python
import jax
import jax.numpy as jnp
from jax import lax
from jax.experimental import pallas as pl
from jax.experimental.pallas import tpu as pltpu
from jax.sharding import PartitionSpec as P

B = 64
K = 5
CS = 8
E = 8
Q = 32
LANES = 128
NX = 4
NZ = 16
NL = 4
TEAM = NX * NL
ROWS = E * K
CODE = 256


F32 = jnp.float32
BF16 = jnp.bfloat16


VMEM = pl.BlockSpec(memory_space=pltpu.VMEM)
SMEM = pl.BlockSpec(memory_space=pltpu.SMEM)


PARAMS = pltpu.CompilerParams(vmem_limit_bytes=24 * 1024 * 1024)


def near(value):
    return pltpu.with_memory_space_constraint(value, pltpu.VMEM)


def low_half(shape):
    return lax.broadcasted_iota(jnp.int32, shape, len(shape) - 1) < B


def two_rows(x, low):
    r = pltpu.roll(x, B, 1)
    return jnp.where(low, x, r), jnp.where(low, r, x)


def product(a2_ref, users, twice):
    low64 = low_half((B, LANES))
    zero = jnp.zeros_like(twice)
    weights = jnp.concatenate(
        [jnp.where(low64, twice, zero), jnp.where(low64, zero, twice)], axis=0
    ).astype(BF16)
    rows = [a2_ref[pl.ds(k * E * Q + e, Q, stride=E), :] for e, k in users]
    left = (rows[0] if len(rows) == 1 else jnp.concatenate(rows, axis=0)).astype(BF16)
    return jnp.dot(left, weights, preferred_element_type=F32).astype(BF16)


def own_kernel(
    agg_hbm, slot_hbm, a_hbm, p_hbm, a2, p2, t2, tags_ref, wd, a_ref, p_ref, agg_ref, slot_ref, sems
):
    pairs = ((agg_hbm, agg_ref), (slot_hbm, slot_ref), (p_hbm, p_ref), (a_hbm, a_ref))
    copies = [pltpu.make_async_copy(*pair, sems.at[i]) for i, pair in enumerate(pairs)]
    for copy in copies:
        copy.start()
    copies[0].wait()
    copies[1].wait()
    place = lax.broadcasted_iota(jnp.int32, (E, LANES), 0) * LANES
    place += lax.broadcasted_iota(jnp.int32, (E, LANES), 1)
    place -= (lax.axis_index("gx") & (TEAM - 1)) * ROWS
    code = jnp.zeros((E, LANES), jnp.int32)
    for e in range(E):
        first = agg_ref[0, e] * CS - CODE
        for k in range(K):
            code = jnp.where(place == e * K + k, first + slot_ref[k, 0, e], code)
    tags_ref[...] = code.astype(F32)
    low8 = low_half((E, LANES))
    copies[2].wait()
    for q in range(Q):
        x = p_ref[:, LANES * q : LANES * (q + 1)].astype(F32)
        p2[E * q : E * (q + 1), :] = x
        even, odd = two_rows(x, low8)
        wd[2 * E * q : 2 * E * q + E, :] = even
        wd[2 * E * q + E : 2 * E * (q + 1), :] = odd
    copies[3].wait()
    for k in range(K):
        for q in range(Q):
            x = a_ref[k, :, LANES * q : LANES * (q + 1)].astype(F32)
            a2[(k * Q + q) * E : (k * Q + q + 1) * E, :] = x
    for e in range(E):
        users = [(e, 0)]
        if e + 1 < E:
            users.append((e + 1, 3))
        if e > 0:
            users.append((e - 1, 4))
        result = product(a2, users, wd[pl.ds(e, B, stride=E), :])
        for place, (user, k) in enumerate(users):
            t2[user, :, LANES * k : LANES * (k + 1)] = result[place * Q : (place + 1) * Q]


def own_products(agg, slot, a, p):
    return pl.pallas_call(
        own_kernel,
        out_shape=(
            pltpu.VMEM((K * E * Q, LANES), F32),
            pltpu.VMEM((E * Q, LANES), F32),
            pltpu.VMEM((E, Q, K * LANES), BF16),
            pltpu.VMEM((E, LANES), F32),
        ),
        in_specs=[pl.BlockSpec(memory_space=pltpu.HBM)] * 4,
        out_specs=(VMEM,) * 4,
        scratch_shapes=[
            pltpu.VMEM((E * B, LANES), F32),
            pltpu.VMEM((K, E, B * B), BF16),
            pltpu.VMEM((E, B * B), BF16),
            pltpu.SMEM((1, E), jnp.int32),
            pltpu.SMEM((K, 1, E), jnp.int32),
            pltpu.SemaphoreType.DMA((4,)),
        ],
        compiler_params=PARAMS,
        name="own_products",
    )(*(pltpu.with_memory_space_constraint(v, pltpu.HBM) for v in (agg, slot, a, p)))


def beside_kernel(a2, p2, t2, tags, ya, yb, xa, xb, out_ref, wd, sums):
    low8 = low_half((E, LANES))
    for number, ref in enumerate((xa, xb, ya, yb)):
        for q in range(Q):
            even, odd = two_rows(ref[:, LANES * q : LANES * (q + 1)].astype(F32), low8)
            base = number * E * B
            wd[base + 2 * E * q : base + 2 * E * q + E, :] = even
            wd[base + 2 * E * q + E : base + 2 * E * (q + 1), :] = odd
    odd_x = lax.axis_index("gx") & 1
    odd_y = lax.axis_index("gy") & 1

    def multiply(number, beside, e, k):
        start = pl.multiple_of(number * E * B, E) + beside
        return product(a2, [(e, k)], wd[pl.ds(start, B, stride=E), :])

    low32 = low_half((Q, LANES))
    for e in range(E):
        parts = [t2[e, :, LANES * k : LANES * (k + 1)] for k in range(K)]
        parts[1] = multiply(1 - odd_x, e, e, 1)
        parts[2] = multiply(odd_x, e, e, 2)
        if e == 0:
            parts[3] = multiply(3 - odd_y, E - 1, e, 3)
        if e == E - 1:
            parts[4] = multiply(2 + odd_y, 0, e, 4)
        pt = jnp.transpose(p2[pl.ds(e, Q, stride=E), :]).astype(BF16)
        g = jnp.dot(pt, jnp.concatenate(parts, axis=1), preferred_element_type=F32)
        for k in range(K):
            u = g[:B, LANES * k : LANES * (k + 1)]
            v = g[B:, LANES * k : LANES * (k + 1)]
            first = u[:Q] + pltpu.roll(v[:Q], B, 1)
            second = pltpu.roll(u[Q:], B, 1) + v[Q:]
            block = jnp.where(low32, first, second)
            for i in range(Q // E):
                start = (i * E * K + e * K + k) * E
                sums[start : start + E, :] = block[i * E : (i + 1) * E]
    for b in range(Q):
        starts = [(b // E * E * K + E * group) * E + b % E for group in range(K)]
        rows = [sums[pl.ds(start, E, stride=E), :] for start in starts]
        start = b % 2 * ROWS
        out_ref[b // 2, start : start + ROWS] = jnp.concatenate(rows, axis=0).astype(BF16)
    for place in range(TEAM):
        out_ref[place, 2 * ROWS :] = tags[...].astype(BF16)


def contributions(own, beside):
    return pl.pallas_call(
        beside_kernel,
        out_shape=pltpu.VMEM((TEAM, 2 * ROWS + E, LANES), BF16),
        in_specs=[VMEM] * 8,
        out_specs=VMEM,
        scratch_shapes=[
            pltpu.VMEM((4 * E * B, LANES), F32),
            pltpu.VMEM((E * K * Q, LANES), F32),
        ],
        compiler_params=PARAMS,
        name="contributions",
    )(*map(near, own), *map(near, beside))


def table_kernel(c_ref, out_ref):
    code = c_ref[0, 2 * ROWS :].astype(F32)
    for source in range(1, TEAM):
        code += c_ref[source, 2 * ROWS :].astype(F32)
    code = code.astype(jnp.int32) + CODE
    halves = [
        c_ref[:, t * ROWS : (t + 1) * ROWS].reshape(TEAM * ROWS, LANES) for t in range(2)
    ]
    rows = jnp.concatenate(halves, axis=1)
    target = lax.broadcasted_iota(jnp.int32, (TEAM * CS, LANES), 0)
    for far in range(NL):
        chosen = [
            (target + far * TEAM * CS == code[i : i + 1]).astype(F32).astype(BF16)
            for i in range(TEAM * ROWS // LANES)
        ]
        total = jnp.dot(jnp.concatenate(chosen, axis=1), rows, preferred_element_type=F32)
        out_ref[far * TEAM : (far + 1) * TEAM] = total.reshape(TEAM, CS, 2 * LANES).astype(BF16)


def table(c):
    return pl.pallas_call(
        table_kernel,
        out_shape=pltpu.VMEM((NL * TEAM, CS, 2 * LANES), BF16),
        in_specs=[VMEM],
        out_specs=VMEM,
        compiler_params=PARAMS,
        name="table",
    )(near(c))


def finish_kernel(r_ref, out_ref):
    low8 = low_half((CS, LANES))
    for pair in range(Q // 2):
        part = r_ref[pair].astype(F32)
        for far in range(1, NL):
            part += r_ref[far * TEAM + pair].astype(F32)
        even = part[:, :LANES]
        odd = part[:, LANES:]
        out_ref[:, LANES * pair : LANES * (pair + 1)] = jnp.where(low8, even, pltpu.roll(odd, B, 1))
        place = pair + Q // 2
        out_ref[:, LANES * place : LANES * (place + 1)] = jnp.where(
            low8, pltpu.roll(even, B, 1), odd
        )


def finish(r):
    return pl.pallas_call(
        finish_kernel,
        out_shape=jax.ShapeDtypeStruct((CS, B * B), F32),
        in_specs=[VMEM],
        out_specs=VMEM,
        compiler_params=PARAMS,
        name="finish",
    )(near(r))


def swaps(count, first):
    pairs = [(i, i + 1) for i in range(first, count - 1, 2)]
    return pairs + [(j, i) for i, j in pairs]


def blocks_of_z(y, block):
    return [(NL * block + l + (NL if y % 2 and l < NL // 2 else 0)) % NZ for l in range(NL)]


def teams(count_y):
    return [
        [(NX * z + x) * count_y + y for z in blocks_of_z(y, block) for x in range(NX)]
        for y in range(count_y)
        for block in range(NL)
    ]


def body(blocks_a, prolong, aggregate, coupling_slot):
    count_x = lax.axis_size("gx")
    count_y = lax.axis_size("gy")
    p = prolong.reshape(E, B * B)
    ya = lax.ppermute(p, "gy", swaps(count_y, 0))
    yb = lax.ppermute(p, "gy", swaps(count_y, 1))
    xa = lax.ppermute(p, "gx", swaps(count_x, 0))
    xb = lax.ppermute(p, "gx", swaps(count_x, 1))
    slots = coupling_slot.transpose(2, 0, 1)
    own = own_products(aggregate, slots, blocks_a.reshape(E, K, B * B).transpose(1, 0, 2), p)
    c = contributions(own, (ya, yb, xa, xb))
    c = lax.all_to_all(c, ("gx", "gy"), 0, 0, axis_index_groups=teams(count_y), tiled=True)
    r = lax.all_to_all(table(c), "gx", 0, 0, tiled=True)
    return finish(r).reshape(1, 1, CS, B * B)


def solution(mesh):
    return jax.shard_map(
        body,
        mesh=mesh,
        in_specs=(
            P("gx", "gy", None, None),
            P("gx", "gy", None),
            P("gx", "gy"),
            P("gx", "gy", None),
        ),
        out_specs=P("gx", "gy", None, None),
        check_vma=False,
    )
```

```python
import jax
import jax.numpy as jnp
from jax import lax
from jax.experimental import pallas as pl
from jax.experimental.pallas import tpu as pltpu
from jax.sharding import PartitionSpec as P

B = 64
K = 5
CS = 8
E = 8
Q = 32
LANES = 128
NX = 4
NZ = 16
NL = 4
TEAM = NX * NL
ROWS = E * K
CODE = 256


F32 = jnp.float32
BF16 = jnp.bfloat16


VMEM = pl.BlockSpec(memory_space=pltpu.VMEM)
SMEM = pl.BlockSpec(memory_space=pltpu.SMEM)


PARAMS = pltpu.CompilerParams(vmem_limit_bytes=24 * 1024 * 1024)


def near(value):
    return pltpu.with_memory_space_constraint(value, pltpu.VMEM)


def low_half(shape):
    return lax.broadcasted_iota(jnp.int32, shape, len(shape) - 1) < B


def two_rows(x, low):
    r = pltpu.roll(x, B, 1)
    return jnp.where(low, x, r), jnp.where(low, r, x)


def product(a2_ref, users, twice):
    low64 = low_half((B, LANES))
    zero = jnp.zeros_like(twice)
    weights = jnp.concatenate(
        [jnp.where(low64, twice, zero), jnp.where(low64, zero, twice)], axis=0
    ).astype(BF16)
    rows = [a2_ref[pl.ds(k * E * Q + e, Q, stride=E), :] for e, k in users]
    left = (rows[0] if len(rows) == 1 else jnp.concatenate(rows, axis=0)).astype(BF16)
    return jnp.dot(left, weights, preferred_element_type=F32).astype(BF16)


def own_kernel(
    agg_hbm, slot_hbm, a_hbm, p_hbm, a2, p2, t2, tags_ref, wd, a_ref, p_ref, agg_ref, slot_ref, sems
):
    pairs = ((agg_hbm, agg_ref), (slot_hbm, slot_ref), (p_hbm, p_ref), (a_hbm, a_ref))
    copies = [pltpu.make_async_copy(*pair, sems.at[i]) for i, pair in enumerate(pairs)]
    for copy in copies:
        copy.start()
    copies[0].wait()
    copies[1].wait()
    place = lax.broadcasted_iota(jnp.int32, (E, LANES), 0) * LANES
    place += lax.broadcasted_iota(jnp.int32, (E, LANES), 1)
    place -= (lax.axis_index("gx") & (TEAM - 1)) * ROWS
    code = jnp.zeros((E, LANES), jnp.int32)
    for e in range(E):
        first = agg_ref[0, e] * CS - CODE
        for k in range(K):
            code = jnp.where(place == e * K + k, first + slot_ref[k, 0, e], code)
    tags_ref[...] = code.astype(F32)
    low8 = low_half((E, LANES))
    copies[2].wait()
    for q in range(Q):
        x = p_ref[:, LANES * q : LANES * (q + 1)].astype(F32)
        p2[E * q : E * (q + 1), :] = x
        even, odd = two_rows(x, low8)
        wd[2 * E * q : 2 * E * q + E, :] = even
        wd[2 * E * q + E : 2 * E * (q + 1), :] = odd
    copies[3].wait()
    for k in range(K):
        for q in range(Q):
            x = a_ref[k, :, LANES * q : LANES * (q + 1)].astype(F32)
            a2[(k * Q + q) * E : (k * Q + q + 1) * E, :] = x
    for e in range(E):
        users = [(e, 0)]
        if e + 1 < E:
            users.append((e + 1, 3))
        if e > 0:
            users.append((e - 1, 4))
        result = product(a2, users, wd[pl.ds(e, B, stride=E), :])
        for place, (user, k) in enumerate(users):
            t2[user, :, LANES * k : LANES * (k + 1)] = result[place * Q : (place + 1) * Q]


def own_products(agg, slot, a, p):
    return pl.pallas_call(
        own_kernel,
        out_shape=(
            pltpu.VMEM((K * E * Q, LANES), F32),
            pltpu.VMEM((E * Q, LANES), F32),
            pltpu.VMEM((E, Q, K * LANES), BF16),
            pltpu.VMEM((E, LANES), F32),
        ),
        in_specs=[pl.BlockSpec(memory_space=pltpu.HBM)] * 4,
        out_specs=(VMEM,) * 4,
        scratch_shapes=[
            pltpu.VMEM((E * B, LANES), F32),
            pltpu.VMEM((K, E, B * B), BF16),
            pltpu.VMEM((E, B * B), BF16),
            pltpu.SMEM((1, E), jnp.int32),
            pltpu.SMEM((K, 1, E), jnp.int32),
            pltpu.SemaphoreType.DMA((4,)),
        ],
        compiler_params=PARAMS,
        name="own_products",
    )(*(pltpu.with_memory_space_constraint(v, pltpu.HBM) for v in (agg, slot, a, p)))


def beside_kernel(a2, p2, t2, tags, ya, yb, xa, xb, out_ref, wd, sums):
    low8 = low_half((E, LANES))
    for number, ref in enumerate((xa, xb, ya, yb)):
        for q in range(Q):
            even, odd = two_rows(ref[:, LANES * q : LANES * (q + 1)].astype(F32), low8)
            base = number * E * B
            wd[base + 2 * E * q : base + 2 * E * q + E, :] = even
            wd[base + 2 * E * q + E : base + 2 * E * (q + 1), :] = odd
    odd_x = lax.axis_index("gx") & 1
    odd_y = lax.axis_index("gy") & 1

    def multiply(number, beside, e, k):
        start = pl.multiple_of(number * E * B, E) + beside
        return product(a2, [(e, k)], wd[pl.ds(start, B, stride=E), :])

    low32 = low_half((Q, LANES))
    beside = []
    for e in range(E):
        edge = {1: multiply(1 - odd_x, e, e, 1), 2: multiply(odd_x, e, e, 2)}
        if e == 0:
            edge[3] = multiply(3 - odd_y, E - 1, e, 3)
        if e == E - 1:
            edge[4] = multiply(2 + odd_y, 0, e, 4)
        beside.append(edge)
    turned = [jnp.transpose(p2[pl.ds(e, Q, stride=E), :]).astype(BF16) for e in range(E)]
    results = []
    for e in range(E):
        parts = [t2[e, :, LANES * k : LANES * (k + 1)] for k in range(K)]
        for k, value in beside[e].items():
            parts[k] = value
        right = jnp.concatenate(parts, axis=1)
        results.append(jnp.dot(turned[e], right, preferred_element_type=F32))
    for e, g in enumerate(results):
        for k in range(K):
            u = g[:B, LANES * k : LANES * (k + 1)]
            v = g[B:, LANES * k : LANES * (k + 1)]
            first = u[:Q] + pltpu.roll(v[:Q], B, 1)
            second = pltpu.roll(u[Q:], B, 1) + v[Q:]
            block = jnp.where(low32, first, second)
            for i in range(Q // E):
                start = (i * E * K + e * K + k) * E
                sums[start : start + E, :] = block[i * E : (i + 1) * E]
    for b in range(Q):
        starts = [(b // E * E * K + E * group) * E + b % E for group in range(K)]
        rows = [sums[pl.ds(start, E, stride=E), :] for start in starts]
        start = b % 2 * ROWS
        out_ref[b // 2, start : start + ROWS] = jnp.concatenate(rows, axis=0).astype(BF16)
    for place in range(TEAM):
        out_ref[place, 2 * ROWS :] = tags[...].astype(BF16)


def contributions(own, beside):
    return pl.pallas_call(
        beside_kernel,
        out_shape=pltpu.VMEM((TEAM, 2 * ROWS + E, LANES), BF16),
        in_specs=[VMEM] * 8,
        out_specs=VMEM,
        scratch_shapes=[
            pltpu.VMEM((4 * E * B, LANES), F32),
            pltpu.VMEM((E * K * Q, LANES), F32),
        ],
        compiler_params=PARAMS,
        name="contributions",
    )(*map(near, own), *map(near, beside))


PLACES = [
    NX * (z + side * NZ // 2) + x for x in range(NX) for z in range(NZ // 2) for side in range(2)
]


def table_kernel(c_ref, out_ref):
    code = c_ref[0, 2 * ROWS :].astype(F32)
    for source in range(1, TEAM):
        code += c_ref[source, 2 * ROWS :].astype(F32)
    code = code.astype(jnp.int32) + CODE
    halves = [
        c_ref[:, t * ROWS : (t + 1) * ROWS].reshape(TEAM * ROWS, LANES) for t in range(2)
    ]
    rows = jnp.concatenate(halves, axis=1)
    target = lax.broadcasted_iota(jnp.int32, (TEAM * CS, LANES), 0)
    for far in range(NL):
        chosen = [
            (target + far * TEAM * CS == code[i : i + 1]).astype(F32).astype(BF16)
            for i in range(TEAM * ROWS // LANES)
        ]
        total = jnp.dot(jnp.concatenate(chosen, axis=1), rows, preferred_element_type=F32)
        for i in range(TEAM):
            block = total[i * CS : (i + 1) * CS].astype(BF16)
            out_ref[PLACES.index(far * TEAM + i)] = block


def table(c):
    return pl.pallas_call(
        table_kernel,
        out_shape=pltpu.VMEM((NL * TEAM, CS, 2 * LANES), BF16),
        in_specs=[VMEM],
        out_specs=VMEM,
        compiler_params=PARAMS,
        name="table",
    )(near(c))


def finish_kernel(r_ref, out_ref):
    low8 = low_half((CS, LANES))
    for pair in range(Q // 2):
        part = r_ref[PLACES.index(pair)].astype(F32)
        for far in range(1, NL):
            part += r_ref[PLACES.index(far * TEAM + pair)].astype(F32)
        even = part[:, :LANES]
        odd = part[:, LANES:]
        out_ref[:, LANES * pair : LANES * (pair + 1)] = jnp.where(low8, even, pltpu.roll(odd, B, 1))
        place = pair + Q // 2
        out_ref[:, LANES * place : LANES * (place + 1)] = jnp.where(
            low8, pltpu.roll(even, B, 1), odd
        )


def finish(r):
    return pl.pallas_call(
        finish_kernel,
        out_shape=jax.ShapeDtypeStruct((CS, B * B), F32),
        in_specs=[VMEM],
        out_specs=VMEM,
        compiler_params=PARAMS,
        name="finish",
    )(near(r))


def swaps(count, first):
    pairs = [(i, i + 1) for i in range(first, count - 1, 2)]
    return pairs + [(j, i) for i, j in pairs]


def blocks_of_z(y, block):
    return [(NL * block + l + (NL if y % 2 and l < NL // 2 else 0)) % NZ for l in range(NL)]


def teams(count_y):
    return [
        [(NX * z + x) * count_y + y for z in blocks_of_z(y, block) for x in range(NX)]
        for y in range(count_y)
        for block in range(NL)
    ]


def body(blocks_a, prolong, aggregate, coupling_slot):
    count_x = lax.axis_size("gx")
    count_y = lax.axis_size("gy")
    p = prolong.reshape(E, B * B)
    ya = lax.ppermute(p, "gy", swaps(count_y, 0))
    yb = lax.ppermute(p, "gy", swaps(count_y, 1))
    xa = lax.ppermute(p, "gx", swaps(count_x, 0))
    xb = lax.ppermute(p, "gx", swaps(count_x, 1))
    slots = coupling_slot.transpose(2, 0, 1)
    own = own_products(aggregate, slots, blocks_a.reshape(E, K, B * B).transpose(1, 0, 2), p)
    c = contributions(own, (ya, yb, xa, xb))
    c = lax.all_to_all(c, ("gx", "gy"), 0, 0, axis_index_groups=teams(count_y), tiled=True)
    r = lax.all_to_all(table(c), "gx", 0, 0, axis_index_groups=[PLACES], tiled=True)
    return finish(r).reshape(1, 1, CS, B * B)


def solution(mesh):
    return jax.shard_map(
        body,
        mesh=mesh,
        in_specs=(
            P("gx", "gy", None, None),
            P("gx", "gy", None),
            P("gx", "gy"),
            P("gx", "gy", None),
        ),
        out_specs=P("gx", "gy", None, None),
        check_vma=False,
    )
```

```python
import jax
import jax.numpy as jnp
from jax import lax
from jax.experimental import pallas as pl
from jax.experimental.pallas import tpu as pltpu
from jax.sharding import PartitionSpec as P

B = 64
K = 5
CS = 8
E = 8
Q = 32
LANES = 128
NX = 4
NZ = 16
NL = 4
TEAM = NX * NL
ROWS = E * K
CODE = 256


F32 = jnp.float32
BF16 = jnp.bfloat16


VMEM = pl.BlockSpec(memory_space=pltpu.VMEM)
SMEM = pl.BlockSpec(memory_space=pltpu.SMEM)


PARAMS = pltpu.CompilerParams(vmem_limit_bytes=24 * 1024 * 1024)


def near(value):
    return pltpu.with_memory_space_constraint(value, pltpu.VMEM)


def low_half(shape):
    return lax.broadcasted_iota(jnp.int32, shape, len(shape) - 1) < B


def two_rows(x, low):
    r = pltpu.roll(x, B, 1)
    return jnp.where(low, x, r), jnp.where(low, r, x)


def product(a2_ref, users, twice):
    low64 = low_half((B, LANES))
    zero = jnp.zeros_like(twice)
    weights = jnp.concatenate(
        [jnp.where(low64, twice, zero), jnp.where(low64, zero, twice)], axis=0
    ).astype(BF16)
    rows = [a2_ref[pl.ds(k * E * Q + e, Q, stride=E), :] for e, k in users]
    left = (rows[0] if len(rows) == 1 else jnp.concatenate(rows, axis=0)).astype(BF16)
    return jnp.dot(left, weights, preferred_element_type=F32).astype(BF16)


def own_kernel(
    agg_hbm, slot_hbm, a_hbm, p_hbm, a2, p2, t2, tags_ref, wd, a_ref, p_ref, agg_ref, slot_ref, sems
):
    pairs = ((agg_hbm, agg_ref), (slot_hbm, slot_ref), (p_hbm, p_ref), (a_hbm, a_ref))
    copies = [pltpu.make_async_copy(*pair, sems.at[i]) for i, pair in enumerate(pairs)]
    for copy in copies:
        copy.start()
    copies[0].wait()
    copies[1].wait()
    place = lax.broadcasted_iota(jnp.int32, (E, LANES), 0) * LANES
    place += lax.broadcasted_iota(jnp.int32, (E, LANES), 1)
    place -= (lax.axis_index("gx") & (TEAM - 1)) * ROWS
    code = jnp.zeros((E, LANES), jnp.int32)
    for e in range(E):
        first = agg_ref[0, e] * CS - CODE
        for k in range(K):
            code = jnp.where(place == e * K + k, first + slot_ref[k, 0, e], code)
    tags_ref[...] = code.astype(F32)
    low8 = low_half((E, LANES))
    copies[2].wait()
    for q in range(Q):
        x = p_ref[:, LANES * q : LANES * (q + 1)].astype(F32)
        p2[E * q : E * (q + 1), :] = x
        even, odd = two_rows(x, low8)
        wd[2 * E * q : 2 * E * q + E, :] = even
        wd[2 * E * q + E : 2 * E * (q + 1), :] = odd
    copies[3].wait()
    for k in range(K):
        for q in range(Q):
            x = a_ref[k, :, LANES * q : LANES * (q + 1)].astype(F32)
            a2[(k * Q + q) * E : (k * Q + q + 1) * E, :] = x
    for e in range(E):
        users = [(e, 0)]
        if e + 1 < E:
            users.append((e + 1, 3))
        if e > 0:
            users.append((e - 1, 4))
        result = product(a2, users, wd[pl.ds(e, B, stride=E), :])
        for place, (user, k) in enumerate(users):
            t2[user, :, LANES * k : LANES * (k + 1)] = result[place * Q : (place + 1) * Q]


def own_products(agg, slot, a, p):
    return pl.pallas_call(
        own_kernel,
        out_shape=(
            pltpu.VMEM((K * E * Q, LANES), F32),
            pltpu.VMEM((E * Q, LANES), F32),
            pltpu.VMEM((E, Q, K * LANES), BF16),
            pltpu.VMEM((E, LANES), F32),
        ),
        in_specs=[pl.BlockSpec(memory_space=pltpu.HBM)] * 4,
        out_specs=(VMEM,) * 4,
        scratch_shapes=[
            pltpu.VMEM((E * B, LANES), F32),
            pltpu.VMEM((K, E, B * B), BF16),
            pltpu.VMEM((E, B * B), BF16),
            pltpu.SMEM((1, E), jnp.int32),
            pltpu.SMEM((K, 1, E), jnp.int32),
            pltpu.SemaphoreType.DMA((4,)),
        ],
        compiler_params=PARAMS,
        name="own_products",
    )(*(pltpu.with_memory_space_constraint(v, pltpu.HBM) for v in (agg, slot, a, p)))


def beside_kernel(a2, p2, t2, tags, ya, yb, xa, xb, out_ref, wd, sums):
    low8 = low_half((E, LANES))
    for number, ref in enumerate((xa, xb, ya, yb)):
        for q in range(Q):
            even, odd = two_rows(ref[:, LANES * q : LANES * (q + 1)].astype(F32), low8)
            base = number * E * B
            wd[base + 2 * E * q : base + 2 * E * q + E, :] = even
            wd[base + 2 * E * q + E : base + 2 * E * (q + 1), :] = odd
    odd_x = lax.axis_index("gx") & 1
    odd_y = lax.axis_index("gy") & 1

    def multiply(number, beside, e, k):
        start = pl.multiple_of(number * E * B, E) + beside
        return product(a2, [(e, k)], wd[pl.ds(start, B, stride=E), :])

    low32 = low_half((Q, LANES))
    beside = []
    for e in range(E):
        edge = {1: multiply(1 - odd_x, e, e, 1), 2: multiply(odd_x, e, e, 2)}
        if e == 0:
            edge[3] = multiply(3 - odd_y, E - 1, e, 3)
        if e == E - 1:
            edge[4] = multiply(2 + odd_y, 0, e, 4)
        beside.append(edge)
    turned = [jnp.transpose(p2[pl.ds(e, Q, stride=E), :]).astype(BF16) for e in range(E)]
    results = []
    for e in range(E):
        parts = [t2[e, :, LANES * k : LANES * (k + 1)] for k in range(K)]
        for k, value in beside[e].items():
            parts[k] = value
        right = jnp.concatenate(parts, axis=1)
        results.append(jnp.dot(turned[e], right, preferred_element_type=F32))
    for e, g in enumerate(results):
        for k in range(K):
            u = g[:B, LANES * k : LANES * (k + 1)]
            v = g[B:, LANES * k : LANES * (k + 1)]
            first = u[:Q] + pltpu.roll(v[:Q], B, 1)
            second = pltpu.roll(u[Q:], B, 1) + v[Q:]
            block = jnp.where(low32, first, second)
            for i in range(Q // E):
                start = (i * E * K + e * K + k) * E
                sums[start : start + E, :] = block[i * E : (i + 1) * E]
    for b in range(Q):
        starts = [(b // E * E * K + E * group) * E + b % E for group in range(K)]
        rows = [sums[pl.ds(start, E, stride=E), :] for start in starts]
        start = b % 2 * ROWS
        out_ref[b // 2, start : start + ROWS] = jnp.concatenate(rows, axis=0).astype(BF16)
    for place in range(TEAM):
        out_ref[place, 2 * ROWS :] = tags[...].astype(BF16)


def contributions(own, beside):
    return pl.pallas_call(
        beside_kernel,
        out_shape=pltpu.VMEM((TEAM, 2 * ROWS + E, LANES), BF16),
        in_specs=[VMEM] * 8,
        out_specs=VMEM,
        scratch_shapes=[
            pltpu.VMEM((4 * E * B, LANES), F32),
            pltpu.VMEM((E * K * Q, LANES), F32),
        ],
        compiler_params=PARAMS,
        name="contributions",
    )(*map(near, own), *map(near, beside))


def table_kernel(c_ref, out_ref):
    code = c_ref[0, 2 * ROWS :].astype(F32)
    for source in range(1, TEAM):
        code += c_ref[source, 2 * ROWS :].astype(F32)
    code = code.astype(jnp.int32) + CODE
    halves = [
        c_ref[:, t * ROWS : (t + 1) * ROWS].reshape(TEAM * ROWS, LANES) for t in range(2)
    ]
    rows = jnp.concatenate(halves, axis=1)
    target = lax.broadcasted_iota(jnp.int32, (TEAM * CS, LANES), 0)
    for far in range(NL):
        chosen = [
            (target + far * TEAM * CS == code[i : i + 1]).astype(F32).astype(BF16)
            for i in range(TEAM * ROWS // LANES)
        ]
        total = jnp.dot(jnp.concatenate(chosen, axis=1), rows, preferred_element_type=F32)
        out_ref[far * TEAM : (far + 1) * TEAM] = total.reshape(TEAM, CS, 2 * LANES).astype(BF16)


def table(c):
    return pl.pallas_call(
        table_kernel,
        out_shape=pltpu.VMEM((NL * TEAM, CS, 2 * LANES), BF16),
        in_specs=[VMEM],
        out_specs=VMEM,
        compiler_params=PARAMS,
        name="table",
    )(near(c))


def finish_kernel(r_ref, out_ref):
    low8 = low_half((CS, LANES))
    for pair in range(Q // 2):
        part = r_ref[pair].astype(F32)
        for far in range(1, NL):
            part += r_ref[far * TEAM + pair].astype(F32)
        even = part[:, :LANES]
        odd = part[:, LANES:]
        out_ref[:, LANES * pair : LANES * (pair + 1)] = jnp.where(low8, even, pltpu.roll(odd, B, 1))
        place = pair + Q // 2
        out_ref[:, LANES * place : LANES * (place + 1)] = jnp.where(
            low8, pltpu.roll(even, B, 1), odd
        )


def finish(r):
    return pl.pallas_call(
        finish_kernel,
        out_shape=jax.ShapeDtypeStruct((CS, B * B), F32),
        in_specs=[VMEM],
        out_specs=VMEM,
        compiler_params=PARAMS,
        name="finish",
    )(near(r))


def swaps(count, first):
    pairs = [(i, i + 1) for i in range(first, count - 1, 2)]
    return pairs + [(j, i) for i, j in pairs]


def blocks_of_z(y, block):
    return [(NL * block + l + (NL if y % 2 and l < NL // 2 else 0)) % NZ for l in range(NL)]


def teams(count_y):
    return [
        [(NX * z + x) * count_y + y for z in blocks_of_z(y, block) for x in range(NX)]
        for y in range(count_y)
        for block in range(NL)
    ]


def body(blocks_a, prolong, aggregate, coupling_slot):
    count_x = lax.axis_size("gx")
    count_y = lax.axis_size("gy")
    p = prolong.reshape(E, B * B)
    ya = lax.ppermute(p, "gy", swaps(count_y, 0))
    yb = lax.ppermute(p, "gy", swaps(count_y, 1))
    xa = lax.ppermute(p, "gx", swaps(count_x, 0))
    xb = lax.ppermute(p, "gx", swaps(count_x, 1))
    slots = coupling_slot.transpose(2, 0, 1)
    own = own_products(aggregate, slots, blocks_a.reshape(E, K, B * B).transpose(1, 0, 2), p)
    c = contributions(own, (ya, yb, xa, xb))
    c = lax.all_to_all(c, ("gx", "gy"), 0, 0, axis_index_groups=teams(count_y), tiled=True)
    r = lax.all_to_all(table(c), "gx", 0, 0, tiled=True)
    return finish(r).reshape(1, 1, CS, B * B)


def solution(mesh):
    return jax.shard_map(
        body,
        mesh=mesh,
        in_specs=(
            P("gx", "gy", None, None),
            P("gx", "gy", None),
            P("gx", "gy"),
            P("gx", "gy", None),
        ),
        out_specs=P("gx", "gy", None, None),
        check_vma=False,
    )
```

```python
import jax
import jax.numpy as jnp
from jax import lax
from jax.experimental import pallas as pl
from jax.experimental.pallas import tpu as pltpu
from jax.sharding import PartitionSpec as P

B = 64
K = 5
CS = 8
E = 8
Q = 32
LANES = 128
NX = 4
NZ = 16
NL = 4
TEAM = NX * NL
ROWS = E * K
CODE = 256


F32 = jnp.float32
BF16 = jnp.bfloat16


VMEM = pl.BlockSpec(memory_space=pltpu.VMEM)
SMEM = pl.BlockSpec(memory_space=pltpu.SMEM)


PARAMS = pltpu.CompilerParams(vmem_limit_bytes=24 * 1024 * 1024)


def near(value):
    return pltpu.with_memory_space_constraint(value, pltpu.VMEM)


def low_half(shape):
    return lax.broadcasted_iota(jnp.int32, shape, len(shape) - 1) < B


def two_rows(x, low):
    r = pltpu.roll(x, B, 1)
    return jnp.where(low, x, r), jnp.where(low, r, x)


def product(a2_ref, users, twice):
    low64 = low_half((B, LANES))
    zero = jnp.zeros_like(twice)
    weights = jnp.concatenate(
        [jnp.where(low64, twice, zero), jnp.where(low64, zero, twice)], axis=0
    ).astype(BF16)
    rows = [a2_ref[pl.ds(k * E * Q + e, Q, stride=E), :] for e, k in users]
    left = (rows[0] if len(rows) == 1 else jnp.concatenate(rows, axis=0)).astype(BF16)
    return jnp.dot(left, weights, preferred_element_type=F32).astype(BF16)


def own_kernel(
    agg_hbm, slot_hbm, a_hbm, p_hbm, a2, p2, t2, tags_ref, wd, a_ref, p_ref, agg_ref, slot_ref, sems
):
    pairs = ((agg_hbm, agg_ref), (slot_hbm, slot_ref), (p_hbm, p_ref), (a_hbm, a_ref))
    copies = [pltpu.make_async_copy(*pair, sems.at[i]) for i, pair in enumerate(pairs)]
    for copy in copies:
        copy.start()
    copies[0].wait()
    copies[1].wait()
    place = lax.broadcasted_iota(jnp.int32, (E, LANES), 0) * LANES
    place += lax.broadcasted_iota(jnp.int32, (E, LANES), 1)
    place -= (lax.axis_index("gx") & (TEAM - 1)) * ROWS
    code = jnp.zeros((E, LANES), jnp.int32)
    for e in range(E):
        first = agg_ref[0, e] * CS - CODE
        for k in range(K):
            code = jnp.where(place == e * K + k, first + slot_ref[k, 0, e], code)
    tags_ref[...] = code.astype(F32)
    low8 = low_half((E, LANES))
    copies[2].wait()
    for q in range(Q):
        x = p_ref[:, LANES * q : LANES * (q + 1)].astype(F32)
        p2[E * q : E * (q + 1), :] = x
        even, odd = two_rows(x, low8)
        wd[2 * E * q : 2 * E * q + E, :] = even
        wd[2 * E * q + E : 2 * E * (q + 1), :] = odd
    copies[3].wait()
    for k in range(K):
        for q in range(Q):
            x = a_ref[k, :, LANES * q : LANES * (q + 1)].astype(F32)
            a2[(k * Q + q) * E : (k * Q + q + 1) * E, :] = x
    for e in range(E):
        users = [(e, 0)]
        if e + 1 < E:
            users.append((e + 1, 3))
        if e > 0:
            users.append((e - 1, 4))
        result = product(a2, users, wd[pl.ds(e, B, stride=E), :])
        for place, (user, k) in enumerate(users):
            t2[user, :, LANES * k : LANES * (k + 1)] = result[place * Q : (place + 1) * Q]


def own_products(agg, slot, a, p):
    return pl.pallas_call(
        own_kernel,
        out_shape=(
            pltpu.VMEM((K * E * Q, LANES), F32),
            pltpu.VMEM((E * Q, LANES), F32),
            pltpu.VMEM((E, Q, K * LANES), BF16),
            pltpu.VMEM((E, LANES), F32),
        ),
        in_specs=[pl.BlockSpec(memory_space=pltpu.HBM)] * 4,
        out_specs=(VMEM,) * 4,
        scratch_shapes=[
            pltpu.VMEM((E * B, LANES), F32),
            pltpu.VMEM((K, E, B * B), BF16),
            pltpu.VMEM((E, B * B), BF16),
            pltpu.SMEM((1, E), jnp.int32),
            pltpu.SMEM((K, 1, E), jnp.int32),
            pltpu.SemaphoreType.DMA((4,)),
        ],
        compiler_params=PARAMS,
        name="own_products",
    )(*(pltpu.with_memory_space_constraint(v, pltpu.HBM) for v in (agg, slot, a, p)))


def beside_kernel(a2, p2, t2, tags, ya, yb, xa, xb, out_ref, wd, sums):
    low8 = low_half((E, LANES))
    for number, ref in enumerate((xa, xb, ya, yb)):
        for q in range(Q):
            even, odd = two_rows(ref[:, LANES * q : LANES * (q + 1)].astype(F32), low8)
            base = number * E * B
            wd[base + 2 * E * q : base + 2 * E * q + E, :] = even
            wd[base + 2 * E * q + E : base + 2 * E * (q + 1), :] = odd
    odd_x = lax.axis_index("gx") & 1
    odd_y = lax.axis_index("gy") & 1

    def multiply(number, beside, e, k):
        start = pl.multiple_of(number * E * B, E) + beside
        return product(a2, [(e, k)], wd[pl.ds(start, B, stride=E), :])

    low32 = low_half((Q, LANES))
    beside = []
    for e in range(E):
        edge = {1: multiply(1 - odd_x, e, e, 1), 2: multiply(odd_x, e, e, 2)}
        if e == 0:
            edge[3] = multiply(3 - odd_y, E - 1, e, 3)
        if e == E - 1:
            edge[4] = multiply(2 + odd_y, 0, e, 4)
        beside.append(edge)
    turned = [jnp.transpose(p2[pl.ds(e, Q, stride=E), :]).astype(BF16) for e in range(E)]
    results = []
    for e in range(E):
        parts = [t2[e, :, LANES * k : LANES * (k + 1)] for k in range(K)]
        for k, value in beside[e].items():
            parts[k] = value
        right = jnp.concatenate(parts, axis=1)
        results.append(jnp.dot(turned[e], right, preferred_element_type=F32))
    for e, g in enumerate(results):
        for k in range(K):
            u = g[:B, LANES * k : LANES * (k + 1)]
            v = g[B:, LANES * k : LANES * (k + 1)]
            first = u[:Q] + pltpu.roll(v[:Q], B, 1)
            second = pltpu.roll(u[Q:], B, 1) + v[Q:]
            block = jnp.where(low32, first, second)
            for i in range(Q // E):
                start = (i * E * K + e * K + k) * E
                sums[start : start + E, :] = block[i * E : (i + 1) * E]
    for b in range(Q):
        starts = [(b // E * E * K + E * group) * E + b % E for group in range(K)]
        rows = [sums[pl.ds(start, E, stride=E), :] for start in starts]
        start = b % 2 * ROWS
        out_ref[b // 2, start : start + ROWS] = jnp.concatenate(rows, axis=0).astype(BF16)
    for place in range(TEAM):
        out_ref[place, 2 * ROWS :] = tags[...].astype(BF16)


def contributions(own, beside):
    return pl.pallas_call(
        beside_kernel,
        out_shape=pltpu.VMEM((TEAM, 2 * ROWS + E, LANES), BF16),
        in_specs=[VMEM] * 8,
        out_specs=VMEM,
        scratch_shapes=[
            pltpu.VMEM((4 * E * B, LANES), F32),
            pltpu.VMEM((E * K * Q, LANES), F32),
        ],
        compiler_params=PARAMS,
        name="contributions",
    )(*map(near, own), *map(near, beside))


PLACES = list(range(NX * NZ))[::-1]


def table_kernel(c_ref, out_ref):
    code = c_ref[0, 2 * ROWS :].astype(F32)
    for source in range(1, TEAM):
        code += c_ref[source, 2 * ROWS :].astype(F32)
    code = code.astype(jnp.int32) + CODE
    halves = [
        c_ref[:, t * ROWS : (t + 1) * ROWS].reshape(TEAM * ROWS, LANES) for t in range(2)
    ]
    rows = jnp.concatenate(halves, axis=1)
    target = lax.broadcasted_iota(jnp.int32, (TEAM * CS, LANES), 0)
    for far in range(NL):
        chosen = [
            (target + far * TEAM * CS == code[i : i + 1]).astype(F32).astype(BF16)
            for i in range(TEAM * ROWS // LANES)
        ]
        total = jnp.dot(jnp.concatenate(chosen, axis=1), rows, preferred_element_type=F32)
        for i in range(TEAM):
            block = total[i * CS : (i + 1) * CS].astype(BF16)
            out_ref[PLACES.index(far * TEAM + i)] = block


def table(c):
    return pl.pallas_call(
        table_kernel,
        out_shape=pltpu.VMEM((NL * TEAM, CS, 2 * LANES), BF16),
        in_specs=[VMEM],
        out_specs=VMEM,
        compiler_params=PARAMS,
        name="table",
    )(near(c))


def finish_kernel(r_ref, out_ref):
    low8 = low_half((CS, LANES))
    for pair in range(Q // 2):
        part = r_ref[PLACES.index(pair)].astype(F32)
        for far in range(1, NL):
            part += r_ref[PLACES.index(far * TEAM + pair)].astype(F32)
        even = part[:, :LANES]
        odd = part[:, LANES:]
        out_ref[:, LANES * pair : LANES * (pair + 1)] = jnp.where(low8, even, pltpu.roll(odd, B, 1))
        place = pair + Q // 2
        out_ref[:, LANES * place : LANES * (place + 1)] = jnp.where(
            low8, pltpu.roll(even, B, 1), odd
        )


def finish(r):
    return pl.pallas_call(
        finish_kernel,
        out_shape=jax.ShapeDtypeStruct((CS, B * B), F32),
        in_specs=[VMEM],
        out_specs=VMEM,
        compiler_params=PARAMS,
        name="finish",
    )(near(r))


def swaps(count, first):
    pairs = [(i, i + 1) for i in range(first, count - 1, 2)]
    return pairs + [(j, i) for i, j in pairs]


def blocks_of_z(y, block):
    return [(NL * block + l + (NL if y % 2 and l < NL // 2 else 0)) % NZ for l in range(NL)]


def teams(count_y):
    return [
        [(NX * z + x) * count_y + y for z in blocks_of_z(y, block) for x in range(NX)]
        for y in range(count_y)
        for block in range(NL)
    ]


def body(blocks_a, prolong, aggregate, coupling_slot):
    count_x = lax.axis_size("gx")
    count_y = lax.axis_size("gy")
    p = prolong.reshape(E, B * B)
    ya = lax.ppermute(p, "gy", swaps(count_y, 0))
    yb = lax.ppermute(p, "gy", swaps(count_y, 1))
    xa = lax.ppermute(p, "gx", swaps(count_x, 0))
    xb = lax.ppermute(p, "gx", swaps(count_x, 1))
    slots = coupling_slot.transpose(2, 0, 1)
    own = own_products(aggregate, slots, blocks_a.reshape(E, K, B * B).transpose(1, 0, 2), p)
    c = contributions(own, (ya, yb, xa, xb))
    c = lax.all_to_all(c, ("gx", "gy"), 0, 0, axis_index_groups=teams(count_y), tiled=True)
    r = lax.all_to_all(table(c), "gx", 0, 0, axis_index_groups=[PLACES], tiled=True)
    return finish(r).reshape(1, 1, CS, B * B)


def solution(mesh):
    return jax.shard_map(
        body,
        mesh=mesh,
        in_specs=(
            P("gx", "gy", None, None),
            P("gx", "gy", None),
            P("gx", "gy"),
            P("gx", "gy", None),
        ),
        out_specs=P("gx", "gy", None, None),
        check_vma=False,
    )
```

```python
import jax
import jax.numpy as jnp
from jax import lax
from jax.experimental import pallas as pl
from jax.experimental.pallas import tpu as pltpu
from jax.sharding import PartitionSpec as P

B = 64
K = 5
CS = 8
E = 8
Q = 32
LANES = 128
NX = 4
NZ = 16
NL = 4
TEAM = NX * NL
ROWS = E * K
CODE = 256


F32 = jnp.float32
BF16 = jnp.bfloat16


VMEM = pl.BlockSpec(memory_space=pltpu.VMEM)
SMEM = pl.BlockSpec(memory_space=pltpu.SMEM)


PARAMS = pltpu.CompilerParams(vmem_limit_bytes=24 * 1024 * 1024)


def near(value):
    return pltpu.with_memory_space_constraint(value, pltpu.VMEM)


def low_half(shape):
    return lax.broadcasted_iota(jnp.int32, shape, len(shape) - 1) < B


def two_rows(x, low):
    r = pltpu.roll(x, B, 1)
    return jnp.where(low, x, r), jnp.where(low, r, x)


def product(a2_ref, users, twice):
    low64 = low_half((B, LANES))
    zero = jnp.zeros_like(twice)
    weights = jnp.concatenate(
        [jnp.where(low64, twice, zero), jnp.where(low64, zero, twice)], axis=0
    ).astype(BF16)
    rows = [a2_ref[pl.ds(k * E * Q + e, Q, stride=E), :] for e, k in users]
    left = (rows[0] if len(rows) == 1 else jnp.concatenate(rows, axis=0)).astype(BF16)
    return jnp.dot(left, weights, preferred_element_type=F32).astype(BF16)


def own_kernel(
    agg_hbm, slot_hbm, a_hbm, p_hbm, a2, p2, t2, tags_ref, wd, a_ref, p_ref, agg_ref, slot_ref, sems
):
    pairs = ((agg_hbm, agg_ref), (slot_hbm, slot_ref), (p_hbm, p_ref), (a_hbm, a_ref))
    copies = [pltpu.make_async_copy(*pair, sems.at[i]) for i, pair in enumerate(pairs)]
    for copy in copies:
        copy.start()
    copies[0].wait()
    copies[1].wait()
    place = lax.broadcasted_iota(jnp.int32, (E, LANES), 0) * LANES
    place += lax.broadcasted_iota(jnp.int32, (E, LANES), 1)
    place -= (lax.axis_index("gx") & (TEAM - 1)) * ROWS
    code = jnp.zeros((E, LANES), jnp.int32)
    for e in range(E):
        first = agg_ref[0, e] * CS - CODE
        for k in range(K):
            code = jnp.where(place == e * K + k, first + slot_ref[k, 0, e], code)
    tags_ref[...] = code.astype(F32)
    low8 = low_half((E, LANES))
    copies[2].wait()
    for q in range(Q):
        x = p_ref[:, LANES * q : LANES * (q + 1)].astype(F32)
        p2[E * q : E * (q + 1), :] = x
        even, odd = two_rows(x, low8)
        wd[2 * E * q : 2 * E * q + E, :] = even
        wd[2 * E * q + E : 2 * E * (q + 1), :] = odd
    copies[3].wait()
    for k in range(K):
        for q in range(Q):
            x = a_ref[k, :, LANES * q : LANES * (q + 1)].astype(F32)
            a2[(k * Q + q) * E : (k * Q + q + 1) * E, :] = x
    for e in range(E):
        users = [(e, 0)]
        if e + 1 < E:
            users.append((e + 1, 3))
        if e > 0:
            users.append((e - 1, 4))
        result = product(a2, users, wd[pl.ds(e, B, stride=E), :])
        for place, (user, k) in enumerate(users):
            t2[user, :, LANES * k : LANES * (k + 1)] = result[place * Q : (place + 1) * Q]


def own_products(agg, slot, a, p):
    return pl.pallas_call(
        own_kernel,
        out_shape=(
            pltpu.VMEM((K * E * Q, LANES), F32),
            pltpu.VMEM((E * Q, LANES), F32),
            pltpu.VMEM((E, Q, K * LANES), BF16),
            pltpu.VMEM((E, LANES), F32),
        ),
        in_specs=[pl.BlockSpec(memory_space=pltpu.HBM)] * 4,
        out_specs=(VMEM,) * 4,
        scratch_shapes=[
            pltpu.VMEM((E * B, LANES), F32),
            pltpu.VMEM((K, E, B * B), BF16),
            pltpu.VMEM((E, B * B), BF16),
            pltpu.SMEM((1, E), jnp.int32),
            pltpu.SMEM((K, 1, E), jnp.int32),
            pltpu.SemaphoreType.DMA((4,)),
        ],
        compiler_params=PARAMS,
        name="own_products",
    )(*(pltpu.with_memory_space_constraint(v, pltpu.HBM) for v in (agg, slot, a, p)))


def beside_kernel(a2, p2, t2, tags, ya, yb, xa, xb, out_ref, wd, sums):
    low8 = low_half((E, LANES))
    for number, ref in enumerate((xa, xb, ya, yb)):
        for q in range(Q):
            even, odd = two_rows(ref[:, LANES * q : LANES * (q + 1)].astype(F32), low8)
            base = number * E * B
            wd[base + 2 * E * q : base + 2 * E * q + E, :] = even
            wd[base + 2 * E * q + E : base + 2 * E * (q + 1), :] = odd
    odd_x = lax.axis_index("gx") & 1
    odd_y = lax.axis_index("gy") & 1

    def multiply(number, beside, e, k):
        start = pl.multiple_of(number * E * B, E) + beside
        return product(a2, [(e, k)], wd[pl.ds(start, B, stride=E), :])

    low32 = low_half((Q, LANES))
    beside = []
    for e in range(E):
        edge = {1: multiply(1 - odd_x, e, e, 1), 2: multiply(odd_x, e, e, 2)}
        if e == 0:
            edge[3] = multiply(3 - odd_y, E - 1, e, 3)
        if e == E - 1:
            edge[4] = multiply(2 + odd_y, 0, e, 4)
        beside.append(edge)
    turned = [jnp.transpose(p2[pl.ds(e, Q, stride=E), :]).astype(BF16) for e in range(E)]
    results = []
    for e in range(E):
        parts = [t2[e, :, LANES * k : LANES * (k + 1)] for k in range(K)]
        for k, value in beside[e].items():
            parts[k] = value
        right = jnp.concatenate(parts, axis=1)
        results.append(jnp.dot(turned[e], right, preferred_element_type=F32))
    for e, g in enumerate(results):
        for k in range(K):
            u = g[:B, LANES * k : LANES * (k + 1)]
            v = g[B:, LANES * k : LANES * (k + 1)]
            first = u[:Q] + pltpu.roll(v[:Q], B, 1)
            second = pltpu.roll(u[Q:], B, 1) + v[Q:]
            block = jnp.where(low32, first, second)
            for i in range(Q // E):
                start = (i * E * K + e * K + k) * E
                sums[start : start + E, :] = block[i * E : (i + 1) * E]
    for b in range(Q):
        starts = [(b // E * E * K + E * group) * E + b % E for group in range(K)]
        rows = [sums[pl.ds(start, E, stride=E), :] for start in starts]
        start = b % 2 * ROWS
        out_ref[b // 2, start : start + ROWS] = jnp.concatenate(rows, axis=0).astype(BF16)
    for place in range(TEAM):
        out_ref[place, 2 * ROWS :] = tags[...].astype(BF16)


def contributions(own, beside):
    return pl.pallas_call(
        beside_kernel,
        out_shape=pltpu.VMEM((TEAM, 2 * ROWS + E, LANES), BF16),
        in_specs=[VMEM] * 8,
        out_specs=VMEM,
        scratch_shapes=[
            pltpu.VMEM((4 * E * B, LANES), F32),
            pltpu.VMEM((E * K * Q, LANES), F32),
        ],
        compiler_params=PARAMS,
        name="contributions",
    )(*map(near, own), *map(near, beside))


PLACES = [(NX * (NZ // 2 + 1) - 1 - i) % (NX * NZ) for i in range(NX * NZ)]


def table_kernel(c_ref, out_ref):
    code = c_ref[0, 2 * ROWS :].astype(F32)
    for source in range(1, TEAM):
        code += c_ref[source, 2 * ROWS :].astype(F32)
    code = code.astype(jnp.int32) + CODE
    halves = [
        c_ref[:, t * ROWS : (t + 1) * ROWS].reshape(TEAM * ROWS, LANES) for t in range(2)
    ]
    rows = jnp.concatenate(halves, axis=1)
    target = lax.broadcasted_iota(jnp.int32, (TEAM * CS, LANES), 0)
    for far in range(NL):
        chosen = [
            (target + far * TEAM * CS == code[i : i + 1]).astype(F32).astype(BF16)
            for i in range(TEAM * ROWS // LANES)
        ]
        total = jnp.dot(jnp.concatenate(chosen, axis=1), rows, preferred_element_type=F32)
        for i in range(TEAM):
            block = total[i * CS : (i + 1) * CS].astype(BF16)
            out_ref[PLACES.index(far * TEAM + i)] = block


def table(c):
    return pl.pallas_call(
        table_kernel,
        out_shape=pltpu.VMEM((NL * TEAM, CS, 2 * LANES), BF16),
        in_specs=[VMEM],
        out_specs=VMEM,
        compiler_params=PARAMS,
        name="table",
    )(near(c))


def finish_kernel(r_ref, out_ref):
    low8 = low_half((CS, LANES))
    for pair in range(Q // 2):
        part = r_ref[PLACES.index(pair)].astype(F32)
        for far in range(1, NL):
            part += r_ref[PLACES.index(far * TEAM + pair)].astype(F32)
        even = part[:, :LANES]
        odd = part[:, LANES:]
        out_ref[:, LANES * pair : LANES * (pair + 1)] = jnp.where(low8, even, pltpu.roll(odd, B, 1))
        place = pair + Q // 2
        out_ref[:, LANES * place : LANES * (place + 1)] = jnp.where(
            low8, pltpu.roll(even, B, 1), odd
        )


def finish(r):
    return pl.pallas_call(
        finish_kernel,
        out_shape=jax.ShapeDtypeStruct((CS, B * B), F32),
        in_specs=[VMEM],
        out_specs=VMEM,
        compiler_params=PARAMS,
        name="finish",
    )(near(r))


def swaps(count, first):
    pairs = [(i, i + 1) for i in range(first, count - 1, 2)]
    return pairs + [(j, i) for i, j in pairs]


def blocks_of_z(y, block):
    return [(NL * block + l + (NL if y % 2 and l < NL // 2 else 0)) % NZ for l in range(NL)]


def teams(count_y):
    return [
        [(NX * z + x) * count_y + y for z in blocks_of_z(y, block) for x in range(NX)]
        for y in range(count_y)
        for block in range(NL)
    ]


def body(blocks_a, prolong, aggregate, coupling_slot):
    count_x = lax.axis_size("gx")
    count_y = lax.axis_size("gy")
    p = prolong.reshape(E, B * B)
    ya = lax.ppermute(p, "gy", swaps(count_y, 0))
    yb = lax.ppermute(p, "gy", swaps(count_y, 1))
    xa = lax.ppermute(p, "gx", swaps(count_x, 0))
    xb = lax.ppermute(p, "gx", swaps(count_x, 1))
    slots = coupling_slot.transpose(2, 0, 1)
    own = own_products(aggregate, slots, blocks_a.reshape(E, K, B * B).transpose(1, 0, 2), p)
    c = contributions(own, (ya, yb, xa, xb))
    c = lax.all_to_all(c, ("gx", "gy"), 0, 0, axis_index_groups=teams(count_y), tiled=True)
    r = lax.all_to_all(table(c), "gx", 0, 0, axis_index_groups=[PLACES], tiled=True)
    return finish(r).reshape(1, 1, CS, B * B)


def solution(mesh):
    return jax.shard_map(
        body,
        mesh=mesh,
        in_specs=(
            P("gx", "gy", None, None),
            P("gx", "gy", None),
            P("gx", "gy"),
            P("gx", "gy", None),
        ),
        out_specs=P("gx", "gy", None, None),
        check_vma=False,
    )
```

```python
import jax
import jax.numpy as jnp
from jax import lax
from jax.experimental import pallas as pl
from jax.experimental.pallas import tpu as pltpu
from jax.sharding import PartitionSpec as P

B = 64
K = 5
CS = 8
E = 8
Q = 32
LANES = 128
NX = 4
NZ = 16
NL = 4
TEAM = NX * NL
ROWS = E * K
CODE = 256


F32 = jnp.float32
BF16 = jnp.bfloat16


VMEM = pl.BlockSpec(memory_space=pltpu.VMEM)
SMEM = pl.BlockSpec(memory_space=pltpu.SMEM)


PARAMS = pltpu.CompilerParams(vmem_limit_bytes=24 * 1024 * 1024)


def near(value):
    return pltpu.with_memory_space_constraint(value, pltpu.VMEM)


def low_half(shape):
    return lax.broadcasted_iota(jnp.int32, shape, len(shape) - 1) < B


def two_rows(x, low):
    r = pltpu.roll(x, B, 1)
    return jnp.where(low, x, r), jnp.where(low, r, x)


def product(a2_ref, users, twice):
    low64 = low_half((B, LANES))
    zero = jnp.zeros_like(twice)
    weights = jnp.concatenate(
        [jnp.where(low64, twice, zero), jnp.where(low64, zero, twice)], axis=0
    ).astype(BF16)
    rows = [a2_ref[pl.ds(k * E * Q + e, Q, stride=E), :] for e, k in users]
    left = (rows[0] if len(rows) == 1 else jnp.concatenate(rows, axis=0)).astype(BF16)
    return jnp.dot(left, weights, preferred_element_type=F32).astype(BF16)


def own_kernel(
    agg_hbm, slot_hbm, a_hbm, p_hbm, a2, p2, t2, tags_ref, wd, a_ref, p_ref, agg_ref, slot_ref, sems
):
    pairs = ((agg_hbm, agg_ref), (slot_hbm, slot_ref), (p_hbm, p_ref), (a_hbm, a_ref))
    copies = [pltpu.make_async_copy(*pair, sems.at[i]) for i, pair in enumerate(pairs)]
    for copy in copies:
        copy.start()
    copies[0].wait()
    copies[1].wait()
    place = lax.broadcasted_iota(jnp.int32, (E, LANES), 0) * LANES
    place += lax.broadcasted_iota(jnp.int32, (E, LANES), 1)
    place -= (lax.axis_index("gx") & (TEAM - 1)) * ROWS
    code = jnp.zeros((E, LANES), jnp.int32)
    for e in range(E):
        first = agg_ref[0, e] * CS - CODE
        for k in range(K):
            code = jnp.where(place == e * K + k, first + slot_ref[k, 0, e], code)
    tags_ref[...] = code.astype(F32)
    low8 = low_half((E, LANES))
    copies[2].wait()
    for q in range(Q):
        x = p_ref[:, LANES * q : LANES * (q + 1)].astype(F32)
        p2[E * q : E * (q + 1), :] = x
        even, odd = two_rows(x, low8)
        wd[2 * E * q : 2 * E * q + E, :] = even
        wd[2 * E * q + E : 2 * E * (q + 1), :] = odd
    copies[3].wait()
    for k in range(K):
        for q in range(Q):
            x = a_ref[k, :, LANES * q : LANES * (q + 1)].astype(F32)
            a2[(k * Q + q) * E : (k * Q + q + 1) * E, :] = x
    for e in range(E):
        users = [(e, 0)]
        if e + 1 < E:
            users.append((e + 1, 3))
        if e > 0:
            users.append((e - 1, 4))
        result = product(a2, users, wd[pl.ds(e, B, stride=E), :])
        for place, (user, k) in enumerate(users):
            t2[user, :, LANES * k : LANES * (k + 1)] = result[place * Q : (place + 1) * Q]


def own_products(agg, slot, a, p):
    return pl.pallas_call(
        own_kernel,
        out_shape=(
            pltpu.VMEM((K * E * Q, LANES), F32),
            pltpu.VMEM((E * Q, LANES), F32),
            pltpu.VMEM((E, Q, K * LANES), BF16),
            pltpu.VMEM((E, LANES), F32),
        ),
        in_specs=[pl.BlockSpec(memory_space=pltpu.HBM)] * 4,
        out_specs=(VMEM,) * 4,
        scratch_shapes=[
            pltpu.VMEM((E * B, LANES), F32),
            pltpu.VMEM((K, E, B * B), BF16),
            pltpu.VMEM((E, B * B), BF16),
            pltpu.SMEM((1, E), jnp.int32),
            pltpu.SMEM((K, 1, E), jnp.int32),
            pltpu.SemaphoreType.DMA((4,)),
        ],
        compiler_params=PARAMS,
        name="own_products",
    )(*(pltpu.with_memory_space_constraint(v, pltpu.HBM) for v in (agg, slot, a, p)))


def beside_kernel(a2, p2, t2, tags, ya, yb, xa, xb, out_ref, wd, sums):
    low8 = low_half((E, LANES))
    for number, ref in enumerate((xa, xb, ya, yb)):
        for q in range(Q):
            even, odd = two_rows(ref[:, LANES * q : LANES * (q + 1)].astype(F32), low8)
            base = number * E * B
            wd[base + 2 * E * q : base + 2 * E * q + E, :] = even
            wd[base + 2 * E * q + E : base + 2 * E * (q + 1), :] = odd
    odd_x = lax.axis_index("gx") & 1
    odd_y = lax.axis_index("gy") & 1

    def multiply(number, beside, e, k):
        start = pl.multiple_of(number * E * B, E) + beside
        return product(a2, [(e, k)], wd[pl.ds(start, B, stride=E), :])

    low32 = low_half((Q, LANES))
    beside = []
    for e in range(E):
        edge = {1: multiply(1 - odd_x, e, e, 1), 2: multiply(odd_x, e, e, 2)}
        if e == 0:
            edge[3] = multiply(3 - odd_y, E - 1, e, 3)
        if e == E - 1:
            edge[4] = multiply(2 + odd_y, 0, e, 4)
        beside.append(edge)
    turned = [jnp.transpose(p2[pl.ds(e, Q, stride=E), :]).astype(BF16) for e in range(E)]
    results = []
    for e in range(E):
        parts = [t2[e, :, LANES * k : LANES * (k + 1)] for k in range(K)]
        for k, value in beside[e].items():
            parts[k] = value
        right = jnp.concatenate(parts, axis=1)
        results.append(jnp.dot(turned[e], right, preferred_element_type=F32))
    for e, g in enumerate(results):
        for k in range(K):
            u = g[:B, LANES * k : LANES * (k + 1)]
            v = g[B:, LANES * k : LANES * (k + 1)]
            first = u[:Q] + pltpu.roll(v[:Q], B, 1)
            second = pltpu.roll(u[Q:], B, 1) + v[Q:]
            block = jnp.where(low32, first, second)
            for i in range(Q // E):
                start = (i * E * K + e * K + k) * E
                sums[start : start + E, :] = block[i * E : (i + 1) * E]
    for b in range(Q):
        starts = [(b // E * E * K + E * group) * E + b % E for group in range(K)]
        rows = [sums[pl.ds(start, E, stride=E), :] for start in starts]
        start = b % 2 * ROWS
        out_ref[b // 2, start : start + ROWS] = jnp.concatenate(rows, axis=0).astype(BF16)
    for place in range(TEAM):
        out_ref[place, 2 * ROWS :] = tags[...].astype(BF16)


def contributions(own, beside):
    return pl.pallas_call(
        beside_kernel,
        out_shape=pltpu.VMEM((TEAM, 2 * ROWS + E, LANES), BF16),
        in_specs=[VMEM] * 8,
        out_specs=VMEM,
        scratch_shapes=[
            pltpu.VMEM((4 * E * B, LANES), F32),
            pltpu.VMEM((E * K * Q, LANES), F32),
        ],
        compiler_params=PARAMS,
        name="contributions",
    )(*map(near, own), *map(near, beside))


PLACES = [(NX * NZ // 2 + i) % (NX * NZ) for i in range(NX * NZ)]


def table_kernel(c_ref, out_ref):
    code = c_ref[0, 2 * ROWS :].astype(F32)
    for source in range(1, TEAM):
        code += c_ref[source, 2 * ROWS :].astype(F32)
    code = code.astype(jnp.int32) + CODE
    halves = [
        c_ref[:, t * ROWS : (t + 1) * ROWS].reshape(TEAM * ROWS, LANES) for t in range(2)
    ]
    rows = jnp.concatenate(halves, axis=1)
    target = lax.broadcasted_iota(jnp.int32, (TEAM * CS, LANES), 0)
    for far in range(NL):
        chosen = [
            (target + far * TEAM * CS == code[i : i + 1]).astype(F32).astype(BF16)
            for i in range(TEAM * ROWS // LANES)
        ]
        total = jnp.dot(jnp.concatenate(chosen, axis=1), rows, preferred_element_type=F32)
        for i in range(TEAM):
            block = total[i * CS : (i + 1) * CS].astype(BF16)
            out_ref[PLACES.index(far * TEAM + i)] = block


def table(c):
    return pl.pallas_call(
        table_kernel,
        out_shape=pltpu.VMEM((NL * TEAM, CS, 2 * LANES), BF16),
        in_specs=[VMEM],
        out_specs=VMEM,
        compiler_params=PARAMS,
        name="table",
    )(near(c))


def finish_kernel(r_ref, out_ref):
    low8 = low_half((CS, LANES))
    for pair in range(Q // 2):
        part = r_ref[PLACES.index(pair)].astype(F32)
        for far in range(1, NL):
            part += r_ref[PLACES.index(far * TEAM + pair)].astype(F32)
        even = part[:, :LANES]
        odd = part[:, LANES:]
        out_ref[:, LANES * pair : LANES * (pair + 1)] = jnp.where(low8, even, pltpu.roll(odd, B, 1))
        place = pair + Q // 2
        out_ref[:, LANES * place : LANES * (place + 1)] = jnp.where(
            low8, pltpu.roll(even, B, 1), odd
        )


def finish(r):
    return pl.pallas_call(
        finish_kernel,
        out_shape=jax.ShapeDtypeStruct((CS, B * B), F32),
        in_specs=[VMEM],
        out_specs=VMEM,
        compiler_params=PARAMS,
        name="finish",
    )(near(r))


def swaps(count, first):
    pairs = [(i, i + 1) for i in range(first, count - 1, 2)]
    return pairs + [(j, i) for i, j in pairs]


def blocks_of_z(y, block):
    return [(NL * block + l + (NL if y % 2 and l < NL // 2 else 0)) % NZ for l in range(NL)]


def teams(count_y):
    return [
        [(NX * z + x) * count_y + y for z in blocks_of_z(y, block) for x in range(NX)]
        for y in range(count_y)
        for block in range(NL)
    ]


def body(blocks_a, prolong, aggregate, coupling_slot):
    count_x = lax.axis_size("gx")
    count_y = lax.axis_size("gy")
    p = prolong.reshape(E, B * B)
    ya = lax.ppermute(p, "gy", swaps(count_y, 0))
    yb = lax.ppermute(p, "gy", swaps(count_y, 1))
    xa = lax.ppermute(p, "gx", swaps(count_x, 0))
    xb = lax.ppermute(p, "gx", swaps(count_x, 1))
    slots = coupling_slot.transpose(2, 0, 1)
    own = own_products(aggregate, slots, blocks_a.reshape(E, K, B * B).transpose(1, 0, 2), p)
    c = contributions(own, (ya, yb, xa, xb))
    c = lax.all_to_all(c, ("gx", "gy"), 0, 0, axis_index_groups=teams(count_y), tiled=True)
    r = lax.all_to_all(table(c), "gx", 0, 0, axis_index_groups=[PLACES], tiled=True)
    return finish(r).reshape(1, 1, CS, B * B)


def solution(mesh):
    return jax.shard_map(
        body,
        mesh=mesh,
        in_specs=(
            P("gx", "gy", None, None),
            P("gx", "gy", None),
            P("gx", "gy"),
            P("gx", "gy", None),
        ),
        out_specs=P("gx", "gy", None, None),
        check_vma=False,
    )
```

```python
import jax
import jax.numpy as jnp
from jax import lax
from jax.experimental import pallas as pl
from jax.experimental.pallas import tpu as pltpu
from jax.sharding import PartitionSpec as P

B = 64
K = 5
CS = 8
E = 8
Q = 32
LANES = 128
NX = 4
NZ = 16
NL = 4
TEAM = NX * NL
ROWS = E * K
CODE = 256


F32 = jnp.float32
BF16 = jnp.bfloat16


VMEM = pl.BlockSpec(memory_space=pltpu.VMEM)
SMEM = pl.BlockSpec(memory_space=pltpu.SMEM)


PARAMS = pltpu.CompilerParams(vmem_limit_bytes=24 * 1024 * 1024)


def near(value):
    return pltpu.with_memory_space_constraint(value, pltpu.VMEM)


def low_half(shape):
    return lax.broadcasted_iota(jnp.int32, shape, len(shape) - 1) < B


def two_rows(x, low):
    r = pltpu.roll(x, B, 1)
    return jnp.where(low, x, r), jnp.where(low, r, x)


def product(a2_ref, users, twice):
    low64 = low_half((B, LANES))
    zero = jnp.zeros_like(twice)
    weights = jnp.concatenate(
        [jnp.where(low64, twice, zero), jnp.where(low64, zero, twice)], axis=0
    ).astype(BF16)
    rows = [a2_ref[pl.ds(k * E * Q + e, Q, stride=E), :] for e, k in users]
    left = (rows[0] if len(rows) == 1 else jnp.concatenate(rows, axis=0)).astype(BF16)
    return jnp.dot(left, weights, preferred_element_type=F32).astype(BF16)


def own_kernel(
    agg_hbm, slot_hbm, a_hbm, p_hbm, a2, p2, t2, tags_ref, wd, a_ref, p_ref, agg_ref, slot_ref, sems
):
    pairs = ((agg_hbm, agg_ref), (slot_hbm, slot_ref), (p_hbm, p_ref), (a_hbm, a_ref))
    copies = [pltpu.make_async_copy(*pair, sems.at[i]) for i, pair in enumerate(pairs)]
    for copy in copies:
        copy.start()
    copies[0].wait()
    copies[1].wait()
    place = lax.broadcasted_iota(jnp.int32, (E, LANES), 0) * LANES
    place += lax.broadcasted_iota(jnp.int32, (E, LANES), 1)
    place -= (lax.axis_index("gx") & (TEAM - 1)) * ROWS
    code = jnp.zeros((E, LANES), jnp.int32)
    for e in range(E):
        first = agg_ref[0, e] * CS - CODE
        for k in range(K):
            code = jnp.where(place == e * K + k, first + slot_ref[k, 0, e], code)
    tags_ref[...] = code.astype(F32)
    low8 = low_half((E, LANES))
    copies[2].wait()
    for q in range(Q):
        x = p_ref[:, LANES * q : LANES * (q + 1)].astype(F32)
        p2[E * q : E * (q + 1), :] = x
        even, odd = two_rows(x, low8)
        wd[2 * E * q : 2 * E * q + E, :] = even
        wd[2 * E * q + E : 2 * E * (q + 1), :] = odd
    copies[3].wait()
    for k in range(K):
        for q in range(Q):
            x = a_ref[k, :, LANES * q : LANES * (q + 1)].astype(F32)
            a2[(k * Q + q) * E : (k * Q + q + 1) * E, :] = x
    for e in range(E):
        users = [(e, 0)]
        if e + 1 < E:
            users.append((e + 1, 3))
        if e > 0:
            users.append((e - 1, 4))
        result = product(a2, users, wd[pl.ds(e, B, stride=E), :])
        for place, (user, k) in enumerate(users):
            t2[user, :, LANES * k : LANES * (k + 1)] = result[place * Q : (place + 1) * Q]


def own_products(agg, slot, a, p):
    return pl.pallas_call(
        own_kernel,
        out_shape=(
            pltpu.VMEM((K * E * Q, LANES), F32),
            pltpu.VMEM((E * Q, LANES), F32),
            pltpu.VMEM((E, Q, K * LANES), BF16),
            pltpu.VMEM((E, LANES), F32),
        ),
        in_specs=[pl.BlockSpec(memory_space=pltpu.HBM)] * 4,
        out_specs=(VMEM,) * 4,
        scratch_shapes=[
            pltpu.VMEM((E * B, LANES), F32),
            pltpu.VMEM((K, E, B * B), BF16),
            pltpu.VMEM((E, B * B), BF16),
            pltpu.SMEM((1, E), jnp.int32),
            pltpu.SMEM((K, 1, E), jnp.int32),
            pltpu.SemaphoreType.DMA((4,)),
        ],
        compiler_params=PARAMS,
        name="own_products",
    )(*(pltpu.with_memory_space_constraint(v, pltpu.HBM) for v in (agg, slot, a, p)))


def beside_kernel(a2, p2, t2, tags, ya, yb, xa, xb, out_ref, wd, sums):
    low8 = low_half((E, LANES))
    for number, ref in enumerate((xa, xb, ya, yb)):
        for q in range(Q):
            even, odd = two_rows(ref[:, LANES * q : LANES * (q + 1)].astype(F32), low8)
            base = number * E * B
            wd[base + 2 * E * q : base + 2 * E * q + E, :] = even
            wd[base + 2 * E * q + E : base + 2 * E * (q + 1), :] = odd
    odd_x = lax.axis_index("gx") & 1
    odd_y = lax.axis_index("gy") & 1

    def multiply(number, beside, e, k):
        start = pl.multiple_of(number * E * B, E) + beside
        return product(a2, [(e, k)], wd[pl.ds(start, B, stride=E), :])

    low32 = low_half((Q, LANES))
    beside = []
    for e in range(E):
        edge = {1: multiply(1 - odd_x, e, e, 1), 2: multiply(odd_x, e, e, 2)}
        if e == 0:
            edge[3] = multiply(3 - odd_y, E - 1, e, 3)
        if e == E - 1:
            edge[4] = multiply(2 + odd_y, 0, e, 4)
        beside.append(edge)
    turned = [jnp.transpose(p2[pl.ds(e, Q, stride=E), :]).astype(BF16) for e in range(E)]
    results = []
    for e in range(E):
        parts = [t2[e, :, LANES * k : LANES * (k + 1)] for k in range(K)]
        for k, value in beside[e].items():
            parts[k] = value
        right = jnp.concatenate(parts, axis=1)
        results.append(jnp.dot(turned[e], right, preferred_element_type=F32))
    for e, g in enumerate(results):
        for k in range(K):
            u = g[:B, LANES * k : LANES * (k + 1)]
            v = g[B:, LANES * k : LANES * (k + 1)]
            first = u[:Q] + pltpu.roll(v[:Q], B, 1)
            second = pltpu.roll(u[Q:], B, 1) + v[Q:]
            block = jnp.where(low32, first, second)
            for i in range(Q // E):
                start = (i * E * K + e * K + k) * E
                sums[start : start + E, :] = block[i * E : (i + 1) * E]
    for b in range(Q):
        starts = [(b // E * E * K + E * group) * E + b % E for group in range(K)]
        rows = [sums[pl.ds(start, E, stride=E), :] for start in starts]
        start = b % 2 * ROWS
        out_ref[b // 2, start : start + ROWS] = jnp.concatenate(rows, axis=0).astype(BF16)
    for place in range(TEAM):
        out_ref[place, 2 * ROWS :] = tags[...].astype(BF16)


def contributions(own, beside):
    return pl.pallas_call(
        beside_kernel,
        out_shape=pltpu.VMEM((TEAM, 2 * ROWS + E, LANES), BF16),
        in_specs=[VMEM] * 8,
        out_specs=VMEM,
        scratch_shapes=[
            pltpu.VMEM((4 * E * B, LANES), F32),
            pltpu.VMEM((E * K * Q, LANES), F32),
        ],
        compiler_params=PARAMS,
        name="contributions",
    )(*map(near, own), *map(near, beside))


PLACES = [(NX * (NZ // 2 + 1) + i) % (NX * NZ) for i in range(NX * NZ)]


def table_kernel(c_ref, out_ref):
    code = c_ref[0, 2 * ROWS :].astype(F32)
    for source in range(1, TEAM):
        code += c_ref[source, 2 * ROWS :].astype(F32)
    code = code.astype(jnp.int32) + CODE
    halves = [
        c_ref[:, t * ROWS : (t + 1) * ROWS].reshape(TEAM * ROWS, LANES) for t in range(2)
    ]
    rows = jnp.concatenate(halves, axis=1)
    target = lax.broadcasted_iota(jnp.int32, (TEAM * CS, LANES), 0)
    for far in range(NL):
        chosen = [
            (target + far * TEAM * CS == code[i : i + 1]).astype(F32).astype(BF16)
            for i in range(TEAM * ROWS // LANES)
        ]
        total = jnp.dot(jnp.concatenate(chosen, axis=1), rows, preferred_element_type=F32)
        for i in range(TEAM):
            block = total[i * CS : (i + 1) * CS].astype(BF16)
            out_ref[PLACES.index(far * TEAM + i)] = block


def table(c):
    return pl.pallas_call(
        table_kernel,
        out_shape=pltpu.VMEM((NL * TEAM, CS, 2 * LANES), BF16),
        in_specs=[VMEM],
        out_specs=VMEM,
        compiler_params=PARAMS,
        name="table",
    )(near(c))


def finish_kernel(r_ref, out_ref):
    low8 = low_half((CS, LANES))
    for pair in range(Q // 2):
        part = r_ref[PLACES.index(pair)].astype(F32)
        for far in range(1, NL):
            part += r_ref[PLACES.index(far * TEAM + pair)].astype(F32)
        even = part[:, :LANES]
        odd = part[:, LANES:]
        out_ref[:, LANES * pair : LANES * (pair + 1)] = jnp.where(low8, even, pltpu.roll(odd, B, 1))
        place = pair + Q // 2
        out_ref[:, LANES * place : LANES * (place + 1)] = jnp.where(
            low8, pltpu.roll(even, B, 1), odd
        )


def finish(r):
    return pl.pallas_call(
        finish_kernel,
        out_shape=jax.ShapeDtypeStruct((CS, B * B), F32),
        in_specs=[VMEM],
        out_specs=VMEM,
        compiler_params=PARAMS,
        name="finish",
    )(near(r))


def swaps(count, first):
    pairs = [(i, i + 1) for i in range(first, count - 1, 2)]
    return pairs + [(j, i) for i, j in pairs]


def blocks_of_z(y, block):
    return [(NL * block + l + (NL if y % 2 and l < NL // 2 else 0)) % NZ for l in range(NL)]


def teams(count_y):
    return [
        [(NX * z + x) * count_y + y for z in blocks_of_z(y, block) for x in range(NX)]
        for y in range(count_y)
        for block in range(NL)
    ]


def body(blocks_a, prolong, aggregate, coupling_slot):
    count_x = lax.axis_size("gx")
    count_y = lax.axis_size("gy")
    p = prolong.reshape(E, B * B)
    ya = lax.ppermute(p, "gy", swaps(count_y, 0))
    yb = lax.ppermute(p, "gy", swaps(count_y, 1))
    xa = lax.ppermute(p, "gx", swaps(count_x, 0))
    xb = lax.ppermute(p, "gx", swaps(count_x, 1))
    slots = coupling_slot.transpose(2, 0, 1)
    own = own_products(aggregate, slots, blocks_a.reshape(E, K, B * B).transpose(1, 0, 2), p)
    c = contributions(own, (ya, yb, xa, xb))
    c = lax.all_to_all(c, ("gx", "gy"), 0, 0, axis_index_groups=teams(count_y), tiled=True)
    r = lax.all_to_all(table(c), "gx", 0, 0, axis_index_groups=[PLACES], tiled=True)
    return finish(r).reshape(1, 1, CS, B * B)


def solution(mesh):
    return jax.shard_map(
        body,
        mesh=mesh,
        in_specs=(
            P("gx", "gy", None, None),
            P("gx", "gy", None),
            P("gx", "gy"),
            P("gx", "gy", None),
        ),
        out_specs=P("gx", "gy", None, None),
        check_vma=False,
    )
```
